32 devices in a mesh: view: 4 (over y, core), slab: 8 (over z, x).
Axes of the slice: x: 2, y: 2, z: 4, core: 2. Of those that a mesh axis runs over, the one named last changes fastest.
Arguments:
- estimate: float32 [2, 128, 128, 1024], P(None, 'slab', 'view'), may hold values from 0.2 to 5
- recorded: bfloat16 [2, 2, 128, 128, 1024], P(None, None, None, 'view', 'slab'), may hold values from 0.19921875 to 5
- psf_lateral: float32 [2, 2, 31], replicated, may hold values from 0.0007 to 1.5, as said below
- psf_axial: float32 [2, 127], replicated, may hold values from 0.0007 to 1.5, as said below
- offsets: int32 [2, 2], replicated, may hold values from -8 to 8, as said below
Outputs:
- updated: float32 [2, 128, 128, 1024], P(None, 'slab', 'view')
The draws below stay inside these ranges and needn't reach their ends.
Inputs may be any that keep to these rules, and one draw needn't show every extreme that they name: offsets[v] is imaging direction v's voxel shift along x and along y; the magnitude 8 occurs with both signs. `psf_lateral`: positive lateral taps. `psf_axial`: positive axial taps.
All inputs are finite; a program needn't handle non-finite values.
Results may differ from the reference program's by a relative error of at most 0.0003.
Values sent between devices are 32-bit elements; how exact they have to be, the bound alone decides.
No kernel may reach another device: no remote copies, remote signals or barrier semaphores. Data moves between devices by JAX's collectives and lax.ppermute only.
A program may use at most 128 MiB of HBM per device.

```python
import math
import jax
import jax.numpy as jnp
from jax import lax

C = 2
V = 2
LT = 31
AT = 127
SHIFT = 8
Z = 128
Y = 1024
HALO = 23
X = 128


def draw_offsets(key, part):
    values = jax.random.randint(key, (V, 2), -SHIFT, SHIFT + 1)
    values = values.at[0, 0].set(SHIFT)
    values = values.at[V - 1, 1].set(-SHIFT)
    return values.astype(jnp.int32)


def peaked_taps(key, shape, count, core_lo, core_hi, wing_width, wing_lo, wing_hi):
    first, second, third = jax.random.split(key, 3)
    places = (jnp.arange(count, dtype=jnp.int32) - (count - 1) // 2).astype(jnp.float32)
    squared = places * places
    sigma = jax.random.uniform(first, shape + (1,), jnp.float32, core_lo, core_hi)
    wing_amount = jax.random.uniform(second, shape + (1,), jnp.float32, wing_lo, wing_hi)
    jitter = jnp.exp(jax.random.uniform(third, shape + (count,), jnp.float32, -0.3, 0.3))
    core = jnp.exp(-squared / (2.0 * sigma * sigma))
    wings = wing_amount * jnp.exp(-squared / (2.0 * wing_width * wing_width))
    return ((core + wings + 0.001) * jitter).astype(jnp.float32)


def draw_psf_lateral(key, part):
    return peaked_taps(jax.random.fold_in(key, 17), (V, 2), LT, 0.8, 1.6, max(LT / 6.0, 2.0), 0.01, 0.03)


def draw_psf_axial(key, part):
    return peaked_taps(jax.random.fold_in(key, 29), (V,), AT, 1.0, 2.5, max(AT / 6.0, 3.0), 0.01, 0.04)


def level_of(stream_key, extent, cuts, low, largest):
    level, own = 1.0, jax.random.fold_in(stream_key, 6)
    for position, shards_of in cuts:
        draws = jnp.exp(jax.random.uniform(jax.random.fold_in(own, position), (shards_of,), jnp.float32, low / len(cuts), largest / len(cuts)))
        level = level * jnp.repeat(draws, extent[position] // shards_of).reshape([-1 if axis == position else 1 for axis in range(len(extent))])
    return level


def setup_inputs(seed: int = 0) -> dict:
    keys = jax.random.split(jax.random.key(seed), 6)
    estimate = jnp.clip(jnp.exp(math.log(5.0) - 3.218876 * jax.random.uniform(keys[0], (C, Z, X, Y), jnp.float32) ** level_of(keys[0], (C, Z, X, Y), ((1, 8), (2, 4)), -0.2, 0.2)), 0.2, 5.0)
    recorded = jnp.clip(jnp.exp(math.log(5.0) - 3.2227897 * jax.random.uniform(keys[1], (V, C, Z, X, Y), jnp.float32) ** level_of(keys[1], (V, C, Z, X, Y), ((3, 4), (4, 8)), -0.2, 0.2)), 0.19921875, 5.0).astype(jnp.bfloat16)
    psf_lateral = draw_psf_lateral(jax.random.fold_in(keys[5], 71), 0)
    psf_axial = draw_psf_axial(jax.random.fold_in(keys[5], 71), 0)
    offsets = draw_offsets(jax.random.fold_in(keys[5], 71), 0)
    return {"estimate": estimate, "recorded": recorded, "psf_lateral": psf_lateral, "psf_axial": psf_axial, "offsets": offsets}


BACKGROUND = 0.05


def unit_taps(weights):
    return weights / jnp.sum(weights)


def taps_along(field, weights, offset, axis_at, margin, adjoint):
    length = field.shape[axis_at]
    centre = (weights.shape[0] - 1) // 2
    widths = [(0, 0)] * field.ndim
    widths[axis_at] = (margin, margin)
    padded = jnp.pad(field, widths)
    summed = jnp.zeros(field.shape, jnp.float32)
    for number in range(weights.shape[0]):
        if adjoint:
            anchor = margin - number - offset + centre
        else:
            anchor = margin + number + offset - centre
        summed = summed + weights[number] * lax.dynamic_slice_in_dim(padded, anchor, length, axis_at)
    return summed


def axial_matrix(weights, length):
    centre = (weights.shape[0] - 1) // 2
    rows_at = jnp.arange(length, dtype=jnp.int32)[:, None]
    cols_at = jnp.arange(length, dtype=jnp.int32)[None, :]
    places = cols_at - rows_at + centre
    levels = jnp.arange(weights.shape[0], dtype=jnp.int32)
    return jnp.sum(jnp.where(places[:, :, None] == levels, weights, 0.0), axis=2)


def reference(estimate, recorded, psf_lateral, psf_axial, offsets):
    summed = jnp.zeros(estimate.shape, jnp.float32)
    for which in range(V):
        along_x = unit_taps(psf_lateral[which, 0])
        along_y = unit_taps(psf_lateral[which, 1])
        along_z = axial_matrix(unit_taps(psf_axial[which]), Z)
        blurred = taps_along(estimate, along_x, offsets[which, 0], 2, HALO, False)
        blurred = taps_along(blurred, along_y, offsets[which, 1], 3, HALO, False)
        blurred = jnp.einsum("oi,cixy->coxy", along_z, blurred, precision=lax.Precision.HIGHEST)
        quotient = recorded[which].astype(jnp.float32) / (blurred + BACKGROUND)
        spread = jnp.einsum("oi,coxy->cixy", along_z, quotient, precision=lax.Precision.HIGHEST)
        spread = taps_along(spread, along_y, offsets[which, 1], 3, HALO, True)
        spread = taps_along(spread, along_x, offsets[which, 0], 2, HALO, True)
        summed = summed + spread
    return estimate * (summed / V)
```

```python
import functools

import jax
import jax.numpy as jnp
from jax import lax
from jax.experimental import pallas as pl
from jax.experimental.pallas import tpu as pltpu
from jax.sharding import PartitionSpec as P

HALO = 23
BACKGROUND = 0.05
HIGHEST = lax.Precision.HIGHEST
LANES = 128
EDGE = 24
F32 = jnp.float32
BF16 = jnp.bfloat16
VMEM_LIMIT = 58 * 1024 * 1024


def with_halo(value, sides, width):
    for axis, dim in sides:
        peers, length = (lax.axis_size(axis), value.shape[dim])
        up = [(i, (i + 1) % peers) for i in range(peers - 1)]
        down = [(j, i) for i, j in up]
        last = lax.slice_in_dim(value, length - width, length, axis=dim)
        leading = lax.slice_in_dim(value, 0, width, axis=dim)
        before = lax.ppermute(last, axis, up)
        after = lax.ppermute(leading, axis, down)
        value = jnp.concatenate([before, value, after], axis=dim)
    return value


def unit_taps(weights):
    return weights / jnp.sum(weights)


def band_table(weights, places):
    levels = jnp.arange(weights.shape[0], dtype=jnp.int32)
    return jnp.sum(jnp.where(places[..., None] == levels, weights, 0.0), axis=-1)


def margin_matrix(weights, offset, length, margin, adjoint):
    centre = (weights.shape[0] - 1) // 2
    outputs = jnp.arange(length, dtype=jnp.int32)[:, None]
    sources = jnp.arange(length + 2 * margin, dtype=jnp.int32)[None, :] - margin
    apart = sources - outputs
    if adjoint:
        apart = -apart
    return band_table(weights, apart - offset + centre)


def blocked_rows(field, weights, offset, width_blk, adjoint):
    extent = field.shape
    blocks = extent[3] // width_blk
    pieces = field.reshape(extent[0], extent[1], extent[2], blocks, width_blk)
    padded = jnp.pad(pieces, ((0, 0), (0, 0), (0, 0), (1, 1), (0, 0)))
    centre = (weights.shape[0] - 1) // 2
    sources = jnp.arange(width_blk, dtype=jnp.int32)[:, None]
    outputs = jnp.arange(width_blk, dtype=jnp.int32)[None, :]
    result = jnp.zeros(pieces.shape, F32)
    for shifted in range(3):
        apart = (shifted - 1) * width_blk + sources - outputs
        if adjoint:
            apart = -apart
        matrix = band_table(weights, apart - offset + centre)
        result = result + jnp.einsum(
            "czxkj,ji->czxki",
            padded[:, :, :, shifted : shifted + blocks],
            matrix,
            precision=HIGHEST,
        )
    return result.reshape(extent)


def general_shards(estimate, recorded, psf_lateral, psf_axial, offsets):
    views_n, planes_n = recorded.shape[0], recorded.shape[2]
    along_x = [unit_taps(psf_lateral[which, 0]) for which in range(views_n)]
    along_y = [unit_taps(psf_lateral[which, 1]) for which in range(views_n)]
    rows_at = jnp.arange(planes_n, dtype=jnp.int32)[:, None]
    cols_at = jnp.arange(planes_n, dtype=jnp.int32)[None, :]
    axial_places = cols_at - rows_at + (psf_axial.shape[1] - 1) // 2
    axial = [band_table(unit_taps(psf_axial[which]), axial_places) for which in range(views_n)]
    x_rows = estimate.shape[2]
    widened = with_halo(estimate, (("view", 2),), HALO)
    blurred = []
    for which in range(views_n):
        across = margin_matrix(along_x[which], offsets[which, 0], x_rows, HALO, False)
        sectioned = jnp.einsum("ab,czby->czay", across, widened, precision=HIGHEST)
        blurred.append(blocked_rows(sectioned, along_y[which], offsets[which, 1], LANES, False))
    columns = lax.all_to_all(jnp.stack(blurred), "slab", split_axis=4, concat_axis=2, tiled=True)
    spread = []
    for which in range(views_n):
        imaged = jnp.einsum("oi,cixy->coxy", axial[which], columns[which], precision=HIGHEST)
        quotient = recorded[which].astype(F32) / (imaged + BACKGROUND)
        spread.append(jnp.einsum("oi,coxy->cixy", axial[which], quotient, precision=HIGHEST))
    planes = lax.all_to_all(jnp.stack(spread), "slab", split_axis=2, concat_axis=4, tiled=True)
    returned = [
        blocked_rows(planes[which], along_y[which], offsets[which, 1], LANES, True)
        for which in range(views_n)
    ]
    fringe = with_halo(jnp.stack(returned), (("view", 3),), HALO)
    summed = jnp.zeros(estimate.shape, F32)
    for which in range(views_n):
        across = margin_matrix(along_x[which], offsets[which, 0], x_rows, HALO, True)
        summed = summed + jnp.einsum("ab,czby->czay", across, fringe[which], precision=HIGHEST)
    return estimate * (summed / views_n)


def params():
    return pltpu.CompilerParams(vmem_limit_bytes=VMEM_LIMIT)


def cost(flops, moved):
    return pl.CostEstimate(flops=flops, bytes_accessed=moved, transcendentals=0)


def upward(value, axis):
    return lax.ppermute(value, axis, [(i, i + 1) for i in range(lax.axis_size(axis) - 1)])


def downward(value, axis):
    return lax.ppermute(value, axis, [(i + 1, i) for i in range(lax.axis_size(axis) - 1)])


def split(value):
    high = value.astype(BF16)
    return high, (value - high.astype(F32)).astype(BF16)


def mm(a, b):
    return jnp.dot(a, b, preferred_element_type=F32)


def tables_kernel(y_taps, z_taps, offs, yh, yl, ah, al, zh, zl, th, tl):
    views, taps = y_taps.shape
    axial = z_taps.shape[1]
    size = LANES
    rows = lax.broadcasted_iota(jnp.int32, (size, size), 0)
    cols = lax.broadcasted_iota(jnp.int32, (size, size), 1)
    halo_row = jnp.where(rows < EDGE, rows - EDGE, rows - EDGE + size)
    halo_col = jnp.where(cols < EDGE, cols - EDGE, cols - EDGE + size)
    for v in range(views):
        shift = offs[v, 1] - (taps - 1) // 2
        lanes = slice(v * size, (v + 1) * size)
        places = [rows - cols - shift, halo_row - cols - shift, cols - rows - shift, halo_col - rows - shift]
        limits = [None, rows < 2 * EDGE, None, cols < 2 * EDGE]
        for n, (place, limit) in enumerate(zip(places, limits)):
            acc = jnp.zeros((size, size), F32)
            for k in range(taps):
                acc = jnp.where(place == k, y_taps[v, k], acc)
            if limit is not None:
                acc = jnp.where(limit, acc, 0.0)
            high, low = split(acc)
            block = slice((n % 2) * size, (n % 2 + 1) * size)
            if n < 2:
                yh[block, lanes] = high
                yl[block, lanes] = low
            else:
                ah[lanes, block] = high
                al[lanes, block] = low
        centre = (axial - 1) // 2

        def taps_of(place):
            def step(k, acc):
                return jnp.where(place == k, z_taps[v, k], acc)

            return lax.fori_loop(0, axial, step, jnp.zeros((size, size), F32))

        zh[v], zl[v] = split(taps_of(cols - rows + centre))
        th[v], tl[v] = split(taps_of(rows - cols + centre))


def make_tables(y_taps, z_taps, offsets):
    smem = pl.BlockSpec(memory_space=pltpu.SMEM)
    vmem = pl.BlockSpec(memory_space=pltpu.VMEM)
    views = y_taps.shape[0]
    wide = jax.ShapeDtypeStruct((2 * LANES, views * LANES), BF16)
    tall = jax.ShapeDtypeStruct((views * LANES, 2 * LANES), BF16)
    deep = jax.ShapeDtypeStruct((views, LANES, LANES), BF16)
    return pl.pallas_call(
        tables_kernel,
        out_shape=(wide, wide, tall, tall, deep, deep, deep, deep),
        in_specs=[smem] * 3,
        out_specs=(vmem,) * 8,
        compiler_params=params(),
        cost_estimate=cost(10_000_000, 1_000_000),
        name="tables",
    )(y_taps, z_taps, offsets)


def swap_kernel(source, target):
    target[0] = jnp.swapaxes(source[0], 0, 1)


def send_blocks(estimate, c, peers):
    _, planes, rows, columns = estimate.shape
    width = columns // peers
    return pl.pallas_call(
        swap_kernel,
        grid=(peers,),
        in_specs=[pl.BlockSpec((1, planes, rows, width), lambda s: (c, 0, 0, s))],
        out_specs=pl.BlockSpec((1, rows, planes, width), lambda s: (s, 0, 0, 0)),
        out_shape=jax.ShapeDtypeStruct((peers, rows, planes, width), F32),
        compiler_params=params(),
        cost_estimate=cost(0, 8 * planes * rows * columns),
        name="send_blocks",
    )(estimate)


def record_kernel(source, target):
    target[0, 0] = jnp.swapaxes(source[0, 0].astype(F32), 0, 1).astype(BF16)


def record_rows(recorded):
    views, colours, planes, rows, width = recorded.shape
    step = 16
    return pl.pallas_call(
        record_kernel,
        grid=(views, colours, planes // step),
        in_specs=[pl.BlockSpec((1, 1, step, rows, width), lambda v, c, z: (v, c, z, 0, 0))],
        out_specs=pl.BlockSpec((1, 1, rows, step, width), lambda v, c, z: (v, c, 0, z, 0)),
        out_shape=jax.ShapeDtypeStruct((views, colours, rows, planes, width), BF16),
        compiler_params=params(),
        cost_estimate=cost(0, 4 * recorded.size),
        name="record_rows",
    )(recorded)


def edges_kernel(source, first, last):
    for x in range(source.shape[1]):
        turned = source[:, x].reshape(-1, source.shape[3]).T
        first[x] = turned[:EDGE]
        last[x] = turned[-EDGE:]


def column_edges(block):
    peers, rows, planes, width = block.shape
    step = 8
    edge = jax.ShapeDtypeStruct((rows, EDGE, peers * planes), F32)
    spec = pl.BlockSpec((step, EDGE, peers * planes), lambda x: (x, 0, 0))
    return pl.pallas_call(
        edges_kernel,
        grid=(rows // step,),
        in_specs=[pl.BlockSpec((peers, step, planes, width), lambda x: (0, x, 0, 0))],
        out_specs=(spec, spec),
        out_shape=(edge, edge),
        compiler_params=params(),
        cost_estimate=cost(0, 4 * block.size),
        name="column_edges",
    )(block)


def correlate_kernel(
    x_taps, offs, left, own, right, edge_l, edge_r, corner_l, corner_r, rec,
    yh, yl, ah, al, zh, zl, th, tl, out_l, out_m, out_r, ext, mid,
):
    views, taps = x_taps.shape
    rows = own.shape[1]
    size = LANES
    reach = (taps - 1) // 2
    group = 4
    zeros_tail = jnp.zeros((size - 2 * EDGE, size), F32)

    def along_y(source, x0, halo, base):
        mains, halos = [], []
        for n in range(group):
            mains.append(source[:, x0 + n].reshape(size, size))
            halos.append(jnp.concatenate([*halo(x0 + n), zeros_tail], axis=0).T)
        whole = jnp.concatenate([jnp.concatenate(mains, 0), jnp.concatenate(halos, 0)], axis=1)
        high, low = split(whole)
        done = mm(high, yh[...]) + mm(low, yh[...]) + mm(high, yl[...])
        for v in range(views):
            ext[v, pl.ds(base + x0, group)] = done[:, v * size : (v + 1) * size].reshape(group, size, size)

    @pl.loop(0, EDGE // group)
    def _(g):
        along_y(left, g * group, lambda x: [corner_l[x]], 0)
        along_y(right, g * group, lambda x: [corner_r[x]], EDGE + rows)

    @pl.loop(0, rows // group)
    def _(g):
        along_y(own, g * group, lambda x: [edge_l[x], edge_r[x]], EDGE)

    part = 32
    for v in range(views):
        weights = [jnp.full((8, size), x_taps[v, k], F32) for k in range(taps)]
        begin = EDGE - reach + offs[v, 0]

        @pl.loop(0, (rows // group) * (size // part))
        def _(n):
            x0 = (n // (size // part)) * group
            z0 = pl.multiple_of((n % (size // part)) * part, part)
            sums = [jnp.zeros((part // 8, 8, size), F32) for _ in range(group)]
            for e in range(taps + group - 1):
                value = ext[v, begin + x0 + e, pl.ds(z0, part)].reshape(part // 8, 8, size)
                for j in range(group):
                    if 0 <= e - j < taps:
                        sums[j] = sums[j] + value * weights[e - j][None]
            for j in range(group):
                mid[v, x0 + j, pl.ds(z0, part)] = sums[j].reshape(part, size)

    @pl.loop(0, rows // group)
    def _(g):
        x0 = g * group
        for v in range(views):
            high, low = split(jnp.concatenate([mid[v, x0 + n] for n in range(group)], axis=1))
            image = mm(zh[v], high) + mm(zh[v], low) + mm(zl[v], high)
            seen = jnp.concatenate([rec[v, 0, x0 + n].astype(F32) for n in range(group)], axis=1)
            high, low = split(seen / (image + BACKGROUND))
            back = mm(th[v], high) + mm(th[v], low) + mm(tl[v], high)
            for n in range(group):
                mid[v, x0 + n] = back[:, n * size : (n + 1) * size]

    @pl.loop(0, 2 * EDGE + rows)
    def _(e):
        for v in range(views):
            ext[v, e] = jnp.zeros((size, size), F32)

    for v in range(views):
        weights = [jnp.full((8, size), x_taps[v, k], F32) for k in range(taps)]
        begin = EDGE - reach + offs[v, 0]

        @pl.loop(0, (rows // group) * (size // part))
        def _(n):
            x0 = (n // (size // part)) * group
            z0 = pl.multiple_of((n % (size // part)) * part, part)
            values = [mid[v, x0 + j, pl.ds(z0, part)].reshape(part // 8, 8, size) for j in range(group)]
            for e in range(taps + group - 1):
                total = ext[v, begin + x0 + e, pl.ds(z0, part)].reshape(part // 8, 8, size)
                for j in range(group):
                    if 0 <= e - j < taps:
                        total = total + values[j] * weights[e - j][None]
                ext[v, begin + x0 + e, pl.ds(z0, part)] = total.reshape(part, size)

    def back_y(target, x0, base):
        both = [
            jnp.concatenate([ext[v, base + x0 + n] for v in range(views)], axis=1) for n in range(group)
        ]
        high, low = split(jnp.concatenate(both, axis=0))
        done = mm(high, ah[...]) + mm(low, ah[...]) + mm(high, al[...])
        for n in range(group):
            piece = done[n * size : (n + 1) * size]
            target[x0 + n, :size] = piece[:, :size]
            target[x0 + n, size:] = piece[:, size:].T[: 2 * EDGE]

    @pl.loop(0, EDGE // group)
    def _(g):
        back_y(out_l, g * group, 0)
        back_y(out_r, g * group, EDGE + rows)

    @pl.loop(0, rows // group)
    def _(g):
        back_y(out_m, g * group, EDGE)


def correlate(c, x_taps, offsets, left, own, right, edge_l, edge_r, corner_l, corner_r, rec, tables):
    smem = pl.BlockSpec(memory_space=pltpu.SMEM)
    vmem = pl.BlockSpec(memory_space=pltpu.VMEM)
    rows = own.shape[1]
    views = x_taps.shape[0]
    tall = LANES + 2 * EDGE
    side = jax.ShapeDtypeStruct((EDGE, tall, LANES), F32)
    rec_spec = pl.BlockSpec((views, 1, rows, LANES, LANES), lambda i: (0, c, 0, 0, 0))
    whole = [smem] * 2 + [vmem] * 7 + [rec_spec] + [vmem] * 8
    return pl.pallas_call(
        correlate_kernel,
        grid=(1,),
        out_shape=(side, jax.ShapeDtypeStruct((rows, tall, LANES), F32), side),
        in_specs=whole,
        out_specs=(vmem,) * 3,
        scratch_shapes=[
            pltpu.VMEM((views, 2 * EDGE + rows, LANES, LANES), F32),
            pltpu.VMEM((views, rows, LANES, LANES), F32),
        ],
        compiler_params=params(),
        cost_estimate=cost(20_000_000_000, 30_000_000),
        name="correlate",
    )(x_taps, offsets, left, own, right, edge_l, edge_r, corner_l, corner_r, rec, *tables)


def gather_kernel(own, from_l, from_r, edge_l, edge_r, target):
    rows, size = own.shape[0], LANES
    gap = jnp.zeros((size - 2 * EDGE, size), F32)
    for x in range(rows):
        total = own[x, :size]
        if x < EDGE:
            total = total + from_l[x, :size]
        if x >= rows - EDGE:
            total = total + from_r[x - rows + EDGE, :size]
        total = total + jnp.concatenate([edge_l[x], gap, edge_r[x]], axis=0).T
        target[:, x] = total.reshape(target.shape[0], target.shape[2], size)


def gather_sums(own, from_l, from_r, edge_l, edge_r, peers):
    rows = own.shape[0]
    planes = LANES // peers
    vmem = pl.BlockSpec(memory_space=pltpu.VMEM)
    return pl.pallas_call(
        gather_kernel,
        out_shape=jax.ShapeDtypeStruct((peers, rows, planes, LANES), F32),
        in_specs=[vmem] * 5,
        out_specs=vmem,
        compiler_params=params(),
        cost_estimate=cost(0, 10_000_000),
        name="gather_sums",
    )(own, from_l, from_r, edge_l, edge_r)


def update(estimate, spread, c, views, held):
    _, planes, rows, columns = estimate.shape
    peers = spread.shape[0]
    width = columns // peers
    block = pl.BlockSpec((1, planes, rows, width), lambda s: (c, 0, 0, s))
    extra = [] if held is None else [held]
    return pl.pallas_call(
        functools.partial(update_kernel, views),
        grid=(peers,),
        in_specs=[pl.BlockSpec((1, rows, planes, width), lambda s: (s, 0, 0, 0)), block]
        + [pl.BlockSpec(memory_space=pl.ANY)] * len(extra),
        out_specs=block,
        out_shape=jax.ShapeDtypeStruct(estimate.shape, F32),
        input_output_aliases={2: 0} if extra else {},
        compiler_params=params(),
        cost_estimate=cost(0, 12 * planes * rows * columns),
        name="update",
    )(spread, estimate, *extra)


def update_kernel(views, spread, estimate, *rest):
    rest[-1][0] = estimate[0] * (jnp.swapaxes(spread[0], 0, 1) / views)


def fast_shards(estimate, recorded, psf_lateral, psf_axial, offsets):
    views, colours = recorded.shape[:2]
    rows = estimate.shape[2]
    peers = lax.axis_size("slab")
    lateral = psf_lateral / jnp.sum(psf_lateral, axis=-1, keepdims=True)
    axial = psf_axial / jnp.sum(psf_axial, axis=-1, keepdims=True)
    x_taps = lateral[:, 0]
    tables = make_tables(lateral[:, 1], axial, offsets)
    rec = record_rows(recorded)
    blocks = [
        lax.all_to_all(send_blocks(estimate, c, peers), "slab", 0, 0, tiled=True) for c in range(colours)
    ]
    result = None
    for c in range(colours):
        own = blocks[c]
        left = upward(own[:, rows - EDGE :], "view")
        right = downward(own[:, :EDGE], "view")
        first, last = column_edges(own)
        edge_l = upward(last, "slab")
        edge_r = downward(first, "slab")
        edges = jnp.concatenate([edge_l, edge_r], axis=1)
        corner_l = upward(edges[rows - EDGE :], "view")
        corner_r = downward(edges[:EDGE], "view")
        to_l, mine, to_r = correlate(
            c, x_taps, offsets, left, own, right, edge_l, edge_r, corner_l, corner_r, rec, tables
        )
        from_l = upward(to_r, "view")
        from_r = downward(to_l, "view")
        margin = mine[:, LANES:].at[:EDGE].add(from_l[:, LANES:])
        margin = margin.at[rows - EDGE :].add(from_r[:, LANES:])
        back_r = downward(margin[:, :EDGE], "slab")
        back_l = upward(margin[:, EDGE:], "slab")
        sums = gather_sums(mine, from_l, from_r, back_l, back_r, peers)
        spread = lax.all_to_all(sums, "slab", 0, 0, tiled=True)
        result = update(estimate, spread, c, views, result)
    return result


def shards(estimate, recorded, psf_lateral, psf_axial, offsets):
    planes, rows, width = recorded.shape[2:]
    fits = planes == LANES and width == LANES and rows % 8 == 0 and rows >= EDGE
    fits = fits and estimate.shape[1] % 16 == 0
    run = fast_shards if fits else general_shards
    return run(estimate, recorded, psf_lateral, psf_axial, offsets)


def solution(mesh):
    in_specs = (P(None, "slab", "view", None), P(None, None, None, "view", "slab"), P(), P(), P())
    out_specs = P(None, "slab", "view", None)
    return jax.shard_map(shards, mesh=mesh, in_specs=in_specs, out_specs=out_specs, check_vma=False)
```

```python
import functools

import jax
import jax.numpy as jnp
from jax import lax
from jax.experimental import pallas as pl
from jax.experimental.pallas import tpu as pltpu
from jax.sharding import PartitionSpec as P

HALO = 23
BACKGROUND = 0.05
HIGHEST = lax.Precision.HIGHEST
LANES = 128
REACH = 15
EDGE = 24
F32 = jnp.float32
BF16 = jnp.bfloat16
VMEM_LIMIT = 58 * 1024 * 1024


def with_halo(value, sides, width):
    for axis, dim in sides:
        peers, length = (lax.axis_size(axis), value.shape[dim])
        up = [(i, (i + 1) % peers) for i in range(peers - 1)]
        down = [(j, i) for i, j in up]
        last = lax.slice_in_dim(value, length - width, length, axis=dim)
        leading = lax.slice_in_dim(value, 0, width, axis=dim)
        before = lax.ppermute(last, axis, up)
        after = lax.ppermute(leading, axis, down)
        value = jnp.concatenate([before, value, after], axis=dim)
    return value


def unit_taps(weights):
    return weights / jnp.sum(weights)


def band_table(weights, places):
    levels = jnp.arange(weights.shape[0], dtype=jnp.int32)
    return jnp.sum(jnp.where(places[..., None] == levels, weights, 0.0), axis=-1)


def margin_matrix(weights, offset, length, margin, adjoint):
    centre = (weights.shape[0] - 1) // 2
    outputs = jnp.arange(length, dtype=jnp.int32)[:, None]
    sources = jnp.arange(length + 2 * margin, dtype=jnp.int32)[None, :] - margin
    apart = sources - outputs
    if adjoint:
        apart = -apart
    return band_table(weights, apart - offset + centre)


def blocked_rows(field, weights, offset, width_blk, adjoint):
    extent = field.shape
    blocks = extent[3] // width_blk
    pieces = field.reshape(extent[0], extent[1], extent[2], blocks, width_blk)
    padded = jnp.pad(pieces, ((0, 0), (0, 0), (0, 0), (1, 1), (0, 0)))
    centre = (weights.shape[0] - 1) // 2
    sources = jnp.arange(width_blk, dtype=jnp.int32)[:, None]
    outputs = jnp.arange(width_blk, dtype=jnp.int32)[None, :]
    result = jnp.zeros(pieces.shape, F32)
    for shifted in range(3):
        apart = (shifted - 1) * width_blk + sources - outputs
        if adjoint:
            apart = -apart
        matrix = band_table(weights, apart - offset + centre)
        result = result + jnp.einsum(
            "czxkj,ji->czxki",
            padded[:, :, :, shifted : shifted + blocks],
            matrix,
            precision=HIGHEST,
        )
    return result.reshape(extent)


def general_shards(estimate, recorded, psf_lateral, psf_axial, offsets):
    views_n, planes_n = recorded.shape[0], recorded.shape[2]
    along_x = [unit_taps(psf_lateral[which, 0]) for which in range(views_n)]
    along_y = [unit_taps(psf_lateral[which, 1]) for which in range(views_n)]
    rows_at = jnp.arange(planes_n, dtype=jnp.int32)[:, None]
    cols_at = jnp.arange(planes_n, dtype=jnp.int32)[None, :]
    axial_places = cols_at - rows_at + (psf_axial.shape[1] - 1) // 2
    axial = [band_table(unit_taps(psf_axial[which]), axial_places) for which in range(views_n)]
    x_rows = estimate.shape[2]
    widened = with_halo(estimate, (("view", 2),), HALO)
    blurred = []
    for which in range(views_n):
        across = margin_matrix(along_x[which], offsets[which, 0], x_rows, HALO, False)
        sectioned = jnp.einsum("ab,czby->czay", across, widened, precision=HIGHEST)
        blurred.append(blocked_rows(sectioned, along_y[which], offsets[which, 1], LANES, False))
    columns = lax.all_to_all(jnp.stack(blurred), "slab", split_axis=4, concat_axis=2, tiled=True)
    spread = []
    for which in range(views_n):
        imaged = jnp.einsum("oi,cixy->coxy", axial[which], columns[which], precision=HIGHEST)
        quotient = recorded[which].astype(F32) / (imaged + BACKGROUND)
        spread.append(jnp.einsum("oi,coxy->cixy", axial[which], quotient, precision=HIGHEST))
    planes = lax.all_to_all(jnp.stack(spread), "slab", split_axis=2, concat_axis=4, tiled=True)
    returned = [
        blocked_rows(planes[which], along_y[which], offsets[which, 1], LANES, True)
        for which in range(views_n)
    ]
    fringe = with_halo(jnp.stack(returned), (("view", 3),), HALO)
    summed = jnp.zeros(estimate.shape, F32)
    for which in range(views_n):
        across = margin_matrix(along_x[which], offsets[which, 0], x_rows, HALO, True)
        summed = summed + jnp.einsum("ab,czby->czay", across, fringe[which], precision=HIGHEST)
    return estimate * (summed / views_n)


def params():
    return pltpu.CompilerParams(vmem_limit_bytes=VMEM_LIMIT)


def cost(micros):
    return pl.CostEstimate(flops=0, bytes_accessed=int(micros * 3_600_000), transcendentals=0)


def upward(value, axis):
    return lax.ppermute(value, axis, [(i, i + 1) for i in range(lax.axis_size(axis) - 1)])


def downward(value, axis):
    return lax.ppermute(value, axis, [(i + 1, i) for i in range(lax.axis_size(axis) - 1)])


def split(value):
    high = value.astype(BF16)
    return high, (value - high.astype(F32)).astype(BF16)


def mm(a, b):
    return jnp.dot(a, b, preferred_element_type=F32)


def parts(value, axis):
    high, low = split(value)
    return jnp.concatenate([high, low, high], axis=axis)


def tables_kernel(taps_xy, z_taps, offs, y_fore, y_back, z_fore, z_back, x_fore, x_back, half):
    views, _, taps = taps_xy.shape
    axial = z_taps.shape[1]
    size = LANES
    rows = lax.broadcasted_iota(jnp.int32, (size, size), 0)
    cols = lax.broadcasted_iota(jnp.int32, (size, size), 1)
    halo_row = jnp.where(rows < EDGE, rows - EDGE, rows - EDGE + size)

    def chosen(place, count, tap):
        def step(k, acc):
            return jnp.where(place == k, tap(k), acc)

        return lax.fori_loop(0, count, step, jnp.zeros(place.shape, F32))

    def store(target, value, where):
        high, low = split(value)
        for p, piece in enumerate((high, high, low)):
            target[where(p)] = piece

    def at(r0, c0, height, width):
        return slice(r0, r0 + height), slice(c0, c0 + width)

    for v in range(views):
        shift = offs[v, 1] - (taps - 1) // 2
        for n in range(2):
            place = (rows if n == 0 else halo_row) - cols - shift
            if n == 1:
                place = jnp.where(rows < 2 * EDGE, place, -1)
            fore = chosen(place, taps, lambda k: taps_xy[v, 1, k])
            store(y_fore, fore, lambda p: at((2 * p + n) * size, v * size, size, size))
            store(y_back, fore.T, lambda p: at((views * p + v) * size, n * size, size, size))
        fore = chosen(cols - rows + (axial - 1) // 2, axial, lambda k: z_taps[v, k])
        store(z_fore, fore, lambda p: (v, *at(0, p * size, size, size)))
        store(z_back, fore.T, lambda p: (v, *at(0, p * size, size, size)))

        height, width = x_fore.shape[1], x_fore.shape[2] // 3
        step = 64
        for r0 in range(0, height, step):
            r = lax.broadcasted_iota(jnp.int32, (step, width), 0) + r0
            q = lax.broadcasted_iota(jnp.int32, (step, width), 1)
            place = jnp.where(r % 8 == q % 8, q // 8 - r // 8, -1)
            fore = chosen(place, taps, lambda k: taps_xy[v, 0, k])
            store(x_fore, fore, lambda p: (v, *at(r0, p * width, step, width)))
            half[r0 : r0 + step] = fore
        for r0 in range(0, height, size):
            back = half[r0 : r0 + size].T
            store(x_back, back, lambda p: (v, *at(0, p * height + r0, width, size)))


def make_tables(lateral, axial, offsets, rows):
    smem = pl.BlockSpec(memory_space=pltpu.SMEM)
    vmem = pl.BlockSpec(memory_space=pltpu.VMEM)
    views = lateral.shape[0]
    window = rows + 32
    shapes = [
        (6 * LANES, views * LANES),
        (3 * views * LANES, 2 * LANES),
        (views, LANES, 3 * LANES),
        (views, LANES, 3 * LANES),
        (views, 8 * rows, 3 * 8 * window),
        (views, 8 * window, 3 * 8 * rows),
    ]
    return pl.pallas_call(
        tables_kernel,
        out_shape=tuple(jax.ShapeDtypeStruct(shape, BF16) for shape in shapes),
        in_specs=[smem] * 3,
        out_specs=(vmem,) * len(shapes),
        compiler_params=params(),
        scratch_shapes=[pltpu.VMEM((8 * rows, 8 * window), F32)],
        cost_estimate=cost(14),
        name="tables",
    )(lateral, axial, offsets)


def swap_kernel(source, target):
    width = target.shape[3]
    for k in range(target.shape[0]):
        target[k] = jnp.swapaxes(source[0, :, :, k * width : (k + 1) * width], 0, 1)


def send_blocks(estimate, c, peers):
    _, planes, rows, columns = estimate.shape
    width = columns // peers
    step = min(4, peers)
    return pl.pallas_call(
        swap_kernel,
        grid=(peers // step,),
        in_specs=[pl.BlockSpec((1, planes, rows, step * width), lambda s: (c, 0, 0, s))],
        out_specs=pl.BlockSpec((step, rows, planes, width), lambda s: (s, 0, 0, 0)),
        out_shape=jax.ShapeDtypeStruct((peers, rows, planes, width), F32),
        compiler_params=params(),
        cost_estimate=cost(3),
        name="send_blocks",
    )(estimate)


def record_kernel(source, target):
    target[0, 0] = jnp.swapaxes(source[0, 0].astype(F32), 0, 1).astype(BF16)


def record_rows(recorded):
    views, colours, planes, rows, width = recorded.shape
    step = 64
    return pl.pallas_call(
        record_kernel,
        grid=(views, colours, planes // step),
        in_specs=[pl.BlockSpec((1, 1, step, rows, width), lambda v, c, z: (v, c, z, 0, 0))],
        out_specs=pl.BlockSpec((1, 1, rows, step, width), lambda v, c, z: (v, c, 0, z, 0)),
        out_shape=jax.ShapeDtypeStruct((views, colours, rows, planes, width), BF16),
        compiler_params=params(),
        cost_estimate=cost(8),
        name="record_rows",
    )(recorded)


def edges_kernel(source, first, last, leading, trailing, block, sems):
    peers, rows, planes, size = block.shape
    arrive = pltpu.make_async_copy(source, block, sems.at[0])
    arrive.start()
    arrive.wait()
    depart = [
        pltpu.make_async_copy(block.at[:, pl.ds(0, EDGE)], leading, sems.at[1]),
        pltpu.make_async_copy(block.at[:, pl.ds(rows - EDGE, EDGE)], trailing, sems.at[2]),
    ]
    for copy in depart:
        copy.start()
    for x in range(rows):
        turned = block[:, x].reshape(peers * planes, size).T
        first[x] = turned[:EDGE]
        last[x] = turned[-EDGE:]
    for copy in depart:
        copy.wait()


def block_edges(block):
    peers, rows, planes, width = block.shape
    hbm = pl.BlockSpec(memory_space=pl.ANY)
    vmem = pl.BlockSpec(memory_space=pltpu.VMEM)
    edge = jax.ShapeDtypeStruct((rows, EDGE, peers * planes), F32)
    side = jax.ShapeDtypeStruct((peers, EDGE, planes, width), F32)
    return pl.pallas_call(
        edges_kernel,
        in_specs=[hbm],
        out_specs=(vmem, vmem, hbm, hbm),
        out_shape=(edge, edge, side, side),
        scratch_shapes=[pltpu.VMEM(block.shape, F32), pltpu.SemaphoreType.DMA((3,))],
        compiler_params=params(),
        cost_estimate=cost(4),
        name="block_edges",
    )(block)


def correlate_kernel(c, count, offs, *rest):
    sources, rest = rest[:count], rest[count:]
    outs, held_in, rest = rest[:3], rest[3 : 3 + count], rest[3 + count :]
    out_l, out_m, out_r = outs
    ext, mid, v_out, arrive, depart = rest
    edge_l, edge_r, own, left, right, corner_l, corner_r = held_in[:7]
    y_fore, x_fore, rec, z_fore, z_back, x_back, y_back = held_in[7:]
    views = rec.shape[0]
    rows = own.shape[1]
    size = LANES
    window = x_back.shape[1] // 8
    group = 4
    wide = 4
    held = ext.shape[1]
    zeros_tail = jnp.zeros((size - 2 * EDGE, size), F32)
    incoming = []
    for n, (source, target) in enumerate(zip(sources, held_in)):
        source = source.at[:, c] if target is rec else source
        incoming.append(pltpu.make_async_copy(source, target, arrive.at[n]))
    order = (7, 0, 1, 2, 3, 4, 5, 6, 8, 9, 10, 11, 12, 13)
    for n in order:
        incoming[n].start()

    def need(*names):
        for n in names:
            incoming[n].wait()

    begin = [EDGE - REACH + offs[v, 0] for v in range(views)]

    def clear(first, last):
        for v in range(views):

            @pl.loop(first, last)
            def _(e):
                ext[v, e] = jnp.zeros((size, size), F32)

    clear(2 * EDGE + rows, held)

    def along_y(main, halo, x0, base):
        mains, halos = [], []
        for n in range(group):
            mains.append(main(x0 + n))
            halos.append(jnp.concatenate([*halo(x0 + n), zeros_tail], axis=0).T)
        whole = jnp.concatenate([jnp.concatenate(mains, 0), jnp.concatenate(halos, 0)], axis=1)
        done = mm(parts(whole, 1), y_fore[...])
        for v in range(views):
            ext[v, pl.ds(base + x0, group)] = done[:, v * size : (v + 1) * size].reshape(group, size, size)

    need(7, 0, 1, 2)

    @pl.loop(0, rows // group)
    def _(g):
        along_y(
            lambda x: own[:, x].reshape(size, size), lambda x: [edge_l[x], edge_r[x]], g * group, EDGE
        )

    need(3, 4, 5, 6)

    @pl.loop(0, EDGE // group)
    def _(g):
        along_y(lambda x: left[:, x].reshape(size, size), lambda x: [corner_l[x]], g * group, 0)
        along_y(
            lambda x: right[:, x].reshape(size, size), lambda x: [corner_r[x]], g * group, EDGE + rows
        )

    need(8)

    @pl.loop(0, size // (8 * wide))
    def _(n):
        z0 = pl.multiple_of(n * 8 * wide, 8 * wide)
        for v in range(views):
            data = jnp.concatenate(
                [
                    ext[v, pl.ds(begin[v], window), pl.ds(z0 + 8 * k, 8)].reshape(8 * window, size)
                    for k in range(wide)
                ],
                axis=1,
            )
            done = mm(x_fore[v], parts(data, 0))
            for k in range(wide):
                mid[v, :, pl.ds(z0 + 8 * k, 8)] = done[:, k * size : (k + 1) * size].reshape(rows, 8, size)

    need(9, 10, 11)

    @pl.loop(0, rows // group)
    def _(g):
        x0 = g * group
        for v in range(views):
            image = mm(z_fore[v], parts(jnp.concatenate([mid[v, x0 + n] for n in range(group)], axis=1), 0))
            seen = jnp.concatenate([rec[v, x0 + n].astype(F32) for n in range(group)], axis=1)
            back = mm(z_back[v], parts(seen / (image + BACKGROUND), 0))
            for n in range(group):
                mid[v, x0 + n] = back[:, n * size : (n + 1) * size]

    need(12)
    clear(0, EDGE)
    clear(EDGE + rows, 2 * EDGE + rows)

    @pl.loop(0, size // (8 * wide))
    def _(n):
        z0 = pl.multiple_of(n * 8 * wide, 8 * wide)
        for v in range(views):
            data = jnp.concatenate(
                [mid[v, :, pl.ds(z0 + 8 * k, 8)].reshape(8 * rows, size) for k in range(wide)], axis=1
            )
            done = mm(x_back[v], parts(data, 0))
            for k in range(wide):
                ext[v, pl.ds(begin[v], window), pl.ds(z0 + 8 * k, 8)] = done[
                    :, k * size : (k + 1) * size
                ].reshape(window, 8, size)

    need(13)
    leaving = []
    for n, (target, base, count) in enumerate(
        [(out_l, 0, EDGE), (out_r, EDGE + rows, EDGE), (out_m, EDGE, rows)]
    ):

        @pl.loop(0, count // group)
        def _(g):
            x0 = g * group
            both = [
                jnp.concatenate([ext[v, base + x0 + k] for v in range(views)], axis=1) for k in range(group)
            ]
            done = mm(parts(jnp.concatenate(both, axis=0), 1), y_back[...])
            for k in range(group):
                piece = done[k * size : (k + 1) * size]
                v_out[base + x0 + k, :size] = piece[:, :size]
                v_out[base + x0 + k, size:] = piece[:, size:].T[: 2 * EDGE]

        leaving.append(pltpu.make_async_copy(v_out.at[pl.ds(base, count)], target, depart.at[n]))
        leaving[-1].start()
    for copy in leaving:
        copy.wait()


def correlate(c, offsets, left, own, right, edge_l, edge_r, corner_l, corner_r, rec, tables):
    smem = pl.BlockSpec(memory_space=pltpu.SMEM)
    hbm = pl.BlockSpec(memory_space=pl.ANY)
    rows = own.shape[1]
    views = rec.shape[0]
    tall = LANES + 2 * EDGE
    side = jax.ShapeDtypeStruct((EDGE, tall, LANES), F32)
    y_fore, y_back, z_fore, z_back, x_fore, x_back = tables
    arrays = edge_l, edge_r, own, left, right, corner_l, corner_r
    arrays += y_fore, x_fore, rec, z_fore, z_back, x_back, y_back
    count = len(arrays)
    held = [
        pltpu.VMEM((views, rows, LANES, LANES), BF16) if a is rec else pltpu.VMEM(a.shape, a.dtype)
        for a in arrays
    ]
    return pl.pallas_call(
        functools.partial(correlate_kernel, c, count),
        out_shape=(side, jax.ShapeDtypeStruct((rows, tall, LANES), F32), side),
        in_specs=[smem] + [hbm] * count,
        out_specs=(hbm,) * 3,
        scratch_shapes=held
        + [
            pltpu.VMEM((views, 2 * EDGE + rows + 8, LANES, LANES), F32),
            pltpu.VMEM((views, rows, LANES, LANES), F32),
            pltpu.VMEM((2 * EDGE + rows, tall, LANES), F32),
            pltpu.SemaphoreType.DMA((count,)),
            pltpu.SemaphoreType.DMA((3,)),
        ],
        compiler_params=params(),
        cost_estimate=cost(32),
        name="correlate",
    )(offsets, *arrays)


def returning_kernel(own, from_l, from_r, first, last, mine, left, right, arrive):
    rows, size = own.shape[0], LANES
    pairs = ((own, mine), (from_l, left), (from_r, right))
    copies = [
        pltpu.make_async_copy(source.at[:, pl.ds(size, 2 * EDGE)], target, arrive.at[n])
        for n, (source, target) in enumerate(pairs)
    ]
    for copy in copies:
        copy.start()
    for copy in copies:
        copy.wait()
    for x in range(rows):
        total = mine[x]
        if x < EDGE:
            total = total + left[x]
        if x >= rows - EDGE:
            total = total + right[x - rows + EDGE]
        first[x] = total[:EDGE]
        last[x] = total[EDGE:]


def returning_columns(own, from_l, from_r):
    hbm = pl.BlockSpec(memory_space=pl.ANY)
    vmem = pl.BlockSpec(memory_space=pltpu.VMEM)
    rows = own.shape[0]
    edge = jax.ShapeDtypeStruct((rows, EDGE, LANES), F32)
    return pl.pallas_call(
        returning_kernel,
        in_specs=[hbm] * 3,
        out_specs=(vmem, vmem),
        out_shape=(edge, edge),
        scratch_shapes=[pltpu.VMEM((count, 2 * EDGE, LANES), F32) for count in (rows, EDGE, EDGE)]
        + [pltpu.SemaphoreType.DMA((3,))],
        compiler_params=params(),
        cost_estimate=cost(2),
        name="returning_columns",
    )(own, from_l, from_r)


def gather_kernel(own, from_l, from_r, edge_l, edge_r, target):
    rows, size = own.shape[0], LANES
    gap = jnp.zeros((size - 2 * EDGE, size), F32)
    for x in range(rows):
        total = own[x, :size]
        if x < EDGE:
            total = total + from_l[x, :size]
        if x >= rows - EDGE:
            total = total + from_r[x - rows + EDGE, :size]
        total = total + jnp.concatenate([edge_l[x], gap, edge_r[x]], axis=0).T
        target[:, x] = total.reshape(target.shape[0], target.shape[2], size)


def gather_sums(own, from_l, from_r, edge_l, edge_r, peers):
    rows = own.shape[0]
    planes = LANES // peers
    vmem = pl.BlockSpec(memory_space=pltpu.VMEM)
    return pl.pallas_call(
        gather_kernel,
        out_shape=jax.ShapeDtypeStruct((peers, rows, planes, LANES), F32),
        in_specs=[vmem] * 5,
        out_specs=vmem,
        compiler_params=params(),
        cost_estimate=cost(5),
        name="gather_sums",
    )(own, from_l, from_r, edge_l, edge_r)


def update(estimate, spread, c, views, held):
    _, planes, rows, columns = estimate.shape
    peers = spread.shape[0]
    width = columns // peers
    step = min(4, peers)
    block = pl.BlockSpec((1, planes, rows, step * width), lambda s: (c, 0, 0, s))
    extra = [] if held is None else [held]
    return pl.pallas_call(
        functools.partial(update_kernel, views),
        grid=(peers // step,),
        in_specs=[pl.BlockSpec((step, rows, planes, width), lambda s: (s, 0, 0, 0)), block]
        + [pl.BlockSpec(memory_space=pl.ANY)] * len(extra),
        out_specs=block,
        out_shape=jax.ShapeDtypeStruct(estimate.shape, F32),
        input_output_aliases={2: 0} if extra else {},
        compiler_params=params(),
        cost_estimate=cost(4),
        name="update",
    )(spread, estimate, *extra)


def update_kernel(views, spread, estimate, *rest):
    width = spread.shape[3]
    for k in range(spread.shape[0]):
        lanes = slice(k * width, (k + 1) * width)
        rest[-1][0, :, :, lanes] = estimate[0, :, :, lanes] * (jnp.swapaxes(spread[k], 0, 1) / views)


def fast_shards(estimate, recorded, psf_lateral, psf_axial, offsets):
    views, colours = recorded.shape[:2]
    rows = estimate.shape[2]
    peers = lax.axis_size("slab")
    lateral = psf_lateral / jnp.sum(psf_lateral, axis=-1, keepdims=True)
    axial = psf_axial / jnp.sum(psf_axial, axis=-1, keepdims=True)
    tables = make_tables(lateral, axial, offsets, rows)
    rec = record_rows(recorded)
    sent = [send_blocks(estimate, c, peers) for c in range(colours)]
    result = None
    pending = None

    def close(c, result, mine, from_l, from_r, back_l, back_r):
        sums = gather_sums(mine, from_l, from_r, back_l, back_r, peers)
        summed = lax.all_to_all(sums, "slab", 0, 0, tiled=True)
        return update(estimate, summed, c, views, result)

    for c in range(colours):
        own = lax.all_to_all(sent[c], "slab", 0, 0, tiled=True)
        if c == 0:
            own, sent, tables, rec = lax.optimization_barrier((own, sent, tables, rec))
        first, last, leading, trailing = block_edges(own)
        edge_l = upward(last, "slab")
        edge_r = downward(first, "slab")
        left = upward(trailing, "view")
        right = downward(leading, "view")
        if c + 1 < colours:
            edge_l, edge_r, left, right, sent = lax.optimization_barrier((edge_l, edge_r, left, right, sent))
        edges = jnp.concatenate([edge_l, edge_r], axis=1)
        end_l, end_r = edges[rows - EDGE :], edges[:EDGE]
        if pending is not None:
            end_l, end_r, pending = lax.optimization_barrier((end_l, end_r, pending))
            first, last = returning_columns(*pending)
            back_r, back_l = downward(first, "slab"), upward(last, "slab")
        corner_l = upward(end_l, "view")
        corner_r = downward(end_r, "view")
        if pending is not None:
            corner_l, corner_r, first, last = lax.optimization_barrier((corner_l, corner_r, first, last))
        to_l, mine, to_r = correlate(
            c, offsets, left, own, right, edge_l, edge_r, corner_l, corner_r, rec, tables
        )
        if pending is not None:
            mine, back_l, back_r = lax.optimization_barrier((mine, back_l, back_r))
            result = close(c - 1, result, *pending, back_l, back_r)
        pending = mine, upward(to_r, "view"), downward(to_l, "view")
    first, last = returning_columns(*pending)
    return close(colours - 1, result, *pending, upward(last, "slab"), downward(first, "slab"))


def shards(estimate, recorded, psf_lateral, psf_axial, offsets):
    planes, rows, width = recorded.shape[2:]
    fits = planes == LANES and width == LANES and rows % 8 == 0 and rows >= EDGE
    fits = fits and estimate.shape[1] % 16 == 0 and psf_lateral.shape[2] == 2 * REACH + 1
    run = fast_shards if fits else general_shards
    return run(estimate, recorded, psf_lateral, psf_axial, offsets)


def solution(mesh):
    in_specs = (P(None, "slab", "view", None), P(None, None, None, "view", "slab"), P(), P(), P())
    out_specs = P(None, "slab", "view", None)
    return jax.shard_map(shards, mesh=mesh, in_specs=in_specs, out_specs=out_specs, check_vma=False)
```

```python
import functools

import jax
import jax.numpy as jnp
from jax import lax
from jax.experimental import pallas as pl
from jax.experimental.pallas import tpu as pltpu
from jax.sharding import PartitionSpec as P

HALO = 23
BACKGROUND = 0.05
HIGHEST = lax.Precision.HIGHEST
LANES = 128
REACH = 15
EDGE = 24
F32 = jnp.float32
BF16 = jnp.bfloat16


def with_halo(value, sides, width):
    for axis, dim in sides:
        peers, length = (lax.axis_size(axis), value.shape[dim])
        up = [(i, (i + 1) % peers) for i in range(peers - 1)]
        down = [(j, i) for i, j in up]
        last = lax.slice_in_dim(value, length - width, length, axis=dim)
        leading = lax.slice_in_dim(value, 0, width, axis=dim)
        before = lax.ppermute(last, axis, up)
        after = lax.ppermute(leading, axis, down)
        value = jnp.concatenate([before, value, after], axis=dim)
    return value


def unit_taps(weights):
    return weights / jnp.sum(weights)


def band_table(weights, places):
    levels = jnp.arange(weights.shape[0], dtype=jnp.int32)
    return jnp.sum(jnp.where(places[..., None] == levels, weights, 0.0), axis=-1)


def margin_matrix(weights, offset, length, margin, adjoint):
    centre = (weights.shape[0] - 1) // 2
    outputs = jnp.arange(length, dtype=jnp.int32)[:, None]
    sources = jnp.arange(length + 2 * margin, dtype=jnp.int32)[None, :] - margin
    apart = sources - outputs
    if adjoint:
        apart = -apart
    return band_table(weights, apart - offset + centre)


def blocked_rows(field, weights, offset, width_blk, adjoint):
    extent = field.shape
    blocks = extent[3] // width_blk
    pieces = field.reshape(extent[0], extent[1], extent[2], blocks, width_blk)
    padded = jnp.pad(pieces, ((0, 0), (0, 0), (0, 0), (1, 1), (0, 0)))
    centre = (weights.shape[0] - 1) // 2
    sources = jnp.arange(width_blk, dtype=jnp.int32)[:, None]
    outputs = jnp.arange(width_blk, dtype=jnp.int32)[None, :]
    result = jnp.zeros(pieces.shape, F32)
    for shifted in range(3):
        apart = (shifted - 1) * width_blk + sources - outputs
        if adjoint:
            apart = -apart
        matrix = band_table(weights, apart - offset + centre)
        result = result + jnp.einsum(
            "czxkj,ji->czxki",
            padded[:, :, :, shifted : shifted + blocks],
            matrix,
            precision=HIGHEST,
        )
    return result.reshape(extent)


def general_shards(estimate, recorded, psf_lateral, psf_axial, offsets):
    views_n, planes_n = recorded.shape[0], recorded.shape[2]
    along_x = [unit_taps(psf_lateral[which, 0]) for which in range(views_n)]
    along_y = [unit_taps(psf_lateral[which, 1]) for which in range(views_n)]
    rows_at = jnp.arange(planes_n, dtype=jnp.int32)[:, None]
    cols_at = jnp.arange(planes_n, dtype=jnp.int32)[None, :]
    axial_places = cols_at - rows_at + (psf_axial.shape[1] - 1) // 2
    axial = [band_table(unit_taps(psf_axial[which]), axial_places) for which in range(views_n)]
    x_rows = estimate.shape[2]
    widened = with_halo(estimate, (("view", 2),), HALO)
    blurred = []
    for which in range(views_n):
        across = margin_matrix(along_x[which], offsets[which, 0], x_rows, HALO, False)
        sectioned = jnp.einsum("ab,czby->czay", across, widened, precision=HIGHEST)
        blurred.append(blocked_rows(sectioned, along_y[which], offsets[which, 1], LANES, False))
    columns = lax.all_to_all(jnp.stack(blurred), "slab", split_axis=4, concat_axis=2, tiled=True)
    spread = []
    for which in range(views_n):
        imaged = jnp.einsum("oi,cixy->coxy", axial[which], columns[which], precision=HIGHEST)
        quotient = recorded[which].astype(F32) / (imaged + BACKGROUND)
        spread.append(jnp.einsum("oi,coxy->cixy", axial[which], quotient, precision=HIGHEST))
    planes = lax.all_to_all(jnp.stack(spread), "slab", split_axis=2, concat_axis=4, tiled=True)
    returned = [
        blocked_rows(planes[which], along_y[which], offsets[which, 1], LANES, True)
        for which in range(views_n)
    ]
    fringe = with_halo(jnp.stack(returned), (("view", 3),), HALO)
    summed = jnp.zeros(estimate.shape, F32)
    for which in range(views_n):
        across = margin_matrix(along_x[which], offsets[which, 0], x_rows, HALO, True)
        summed = summed + jnp.einsum("ab,czby->czay", across, fringe[which], precision=HIGHEST)
    return estimate * (summed / views_n)


def params(mebibytes=20):
    return pltpu.CompilerParams(vmem_limit_bytes=mebibytes * 1024 * 1024)


def cost(micros):
    return pl.CostEstimate(flops=0, bytes_accessed=int(micros * 3_600_000), transcendentals=0)


def upward(value, axis):
    return lax.ppermute(value, axis, [(i, i + 1) for i in range(lax.axis_size(axis) - 1)])


def downward(value, axis):
    return lax.ppermute(value, axis, [(i + 1, i) for i in range(lax.axis_size(axis) - 1)])


def after(value, *earlier):
    return lax.optimization_barrier((value, earlier))[0]


def split(value):
    high = value.astype(BF16)
    return high, (value - high.astype(F32)).astype(BF16)


def mm(a, b):
    return jnp.dot(a, b, preferred_element_type=F32)


def parts(value, axis):
    high, low = split(value)
    return jnp.concatenate([high, low, high], axis=axis)


def tables_kernel(taps_xy, z_taps, offs, y_fore, y_back, z_fore, z_back, x_fore, x_back, half):
    views, _, taps = taps_xy.shape
    axial = z_taps.shape[1]
    size = LANES
    rows = lax.broadcasted_iota(jnp.int32, (size, size), 0)
    cols = lax.broadcasted_iota(jnp.int32, (size, size), 1)
    halo_row = jnp.where(rows < EDGE, rows - EDGE, rows - EDGE + size)

    def chosen(place, count, tap):
        def step(k, acc):
            return jnp.where(place == k, tap(k), acc)

        return lax.fori_loop(0, count, step, jnp.zeros(place.shape, F32))

    def store(target, value, where):
        high, low = split(value)
        for p, piece in enumerate((high, high, low)):
            target[where(p)] = piece

    def at(r0, c0, height, width):
        return slice(r0, r0 + height), slice(c0, c0 + width)

    for v in range(views):
        shift = offs[v, 1] - (taps - 1) // 2
        for n in range(2):
            place = (rows if n == 0 else halo_row) - cols - shift
            if n == 1:
                place = jnp.where(rows < 2 * EDGE, place, -1)
            fore = chosen(place, taps, lambda k: taps_xy[v, 1, k])
            store(y_fore, fore, lambda p: at((2 * p + n) * size, v * size, size, size))
            store(y_back, fore.T, lambda p: at((views * p + v) * size, n * size, size, size))
        fore = chosen(cols - rows + (axial - 1) // 2, axial, lambda k: z_taps[v, k])
        store(z_fore, fore, lambda p: (v, *at(0, p * size, size, size)))
        store(z_back, fore.T, lambda p: (v, *at(0, p * size, size, size)))

        height, width = x_fore.shape[1], x_fore.shape[2] // 3
        step = 64
        for r0 in range(0, height, step):
            r = lax.broadcasted_iota(jnp.int32, (step, width), 0) + r0
            q = lax.broadcasted_iota(jnp.int32, (step, width), 1)
            place = jnp.where(r % 8 == q % 8, q // 8 - r // 8, -1)
            fore = chosen(place, taps, lambda k: taps_xy[v, 0, k])
            store(x_fore, fore, lambda p: (v, *at(r0, p * width, step, width)))
            half[r0 : r0 + step] = fore
        for r0 in range(0, height, size):
            back = half[r0 : r0 + size].T
            store(x_back, back, lambda p: (v, *at(0, p * height + r0, width, size)))


def make_tables(lateral, axial, offsets, rows):
    smem = pl.BlockSpec(memory_space=pltpu.SMEM)
    vmem = pl.BlockSpec(memory_space=pltpu.VMEM)
    views = lateral.shape[0]
    window = rows + 32
    shapes = [
        (6 * LANES, views * LANES),
        (3 * views * LANES, 2 * LANES),
        (views, LANES, 3 * LANES),
        (views, LANES, 3 * LANES),
        (views, 8 * rows, 3 * 8 * window),
        (views, 8 * window, 3 * 8 * rows),
    ]
    return pl.pallas_call(
        tables_kernel,
        out_shape=tuple(jax.ShapeDtypeStruct(shape, BF16) for shape in shapes),
        in_specs=[smem] * 3,
        out_specs=(vmem,) * len(shapes),
        compiler_params=params(),
        scratch_shapes=[pltpu.VMEM((8 * rows, 8 * window), F32)],
        cost_estimate=cost(14),
        name="tables",
    )(lateral, axial, offsets)


def swap_kernel(source, target):
    width = target.shape[3]
    for k in range(target.shape[0]):
        target[k] = jnp.swapaxes(source[0, :, :, k * width : (k + 1) * width], 0, 1)


def send_blocks(estimate, c, peers):
    _, planes, rows, columns = estimate.shape
    width = columns // peers
    step = min(4, peers)
    return pl.pallas_call(
        swap_kernel,
        grid=(peers // step,),
        in_specs=[pl.BlockSpec((1, planes, rows, step * width), lambda s: (c, 0, 0, s))],
        out_specs=pl.BlockSpec((step, rows, planes, width), lambda s: (s, 0, 0, 0)),
        out_shape=jax.ShapeDtypeStruct((peers, rows, planes, width), F32),
        compiler_params=params(),
        cost_estimate=cost(3),
        name="send_blocks",
    )(estimate)


def record_kernel(source, target):
    target[0, 0] = jnp.swapaxes(source[0, 0].astype(F32), 0, 1).astype(BF16)


def record_rows(recorded):
    views, colours, planes, rows, width = recorded.shape
    step = 64
    return pl.pallas_call(
        record_kernel,
        grid=(views, colours, planes // step),
        in_specs=[pl.BlockSpec((1, 1, step, rows, width), lambda v, c, z: (v, c, z, 0, 0))],
        out_specs=pl.BlockSpec((1, 1, rows, step, width), lambda v, c, z: (v, c, 0, z, 0)),
        out_shape=jax.ShapeDtypeStruct((views, colours, rows, planes, width), BF16),
        compiler_params=params(),
        cost_estimate=cost(8),
        name="record_rows",
    )(recorded)


def edges_kernel(block, first, last, leading, trailing, sems):
    peers, rows, planes, size = block.shape
    depart = [
        pltpu.make_async_copy(block.at[:, pl.ds(0, EDGE)], leading, sems.at[0]),
        pltpu.make_async_copy(block.at[:, pl.ds(rows - EDGE, EDGE)], trailing, sems.at[1]),
    ]
    for copy in depart:
        copy.start()
    for x in range(rows):
        turned = block[:, x].reshape(peers * planes, size).T
        first[x] = turned[:EDGE]
        last[x] = turned[-EDGE:]
    for copy in depart:
        copy.wait()


def block_edges(block):
    peers, rows, planes, width = block.shape
    hbm = pl.BlockSpec(memory_space=pltpu.HBM)
    vmem = pl.BlockSpec(memory_space=pltpu.VMEM)
    edge = jax.ShapeDtypeStruct((rows, EDGE, peers * planes), F32)
    side = jax.ShapeDtypeStruct((peers, EDGE, planes, width), F32)
    return pl.pallas_call(
        edges_kernel,
        in_specs=[vmem],
        out_specs=(vmem, vmem, hbm, hbm),
        out_shape=(edge, edge, side, side),
        scratch_shapes=[pltpu.SemaphoreType.DMA((2,))],
        compiler_params=params(),
        cost_estimate=cost(4),
        name="block_edges",
    )(block)


def correlate_kernel(c, count, offs, edge_l, edge_r, own, left, right, corner_l, corner_r, *rest):
    sources, rest = rest[:count], rest[count:]
    (out_l, out_m, out_r), held_in, rest = rest[:3], rest[3 : 3 + count], rest[3 + count :]
    ext, mid, v_out, arrive, depart = rest
    y_fore, x_fore, rec, z_fore, z_back, x_back, y_back = held_in
    views = rec.shape[0]
    rows = own.shape[1]
    size = LANES
    window = x_back.shape[1] // 8
    group = 8
    wide = 4
    held = ext.shape[1]
    zeros_tail = jnp.zeros((size - 2 * EDGE, size), F32)
    incoming = []
    for n, (source, target) in enumerate(zip(sources, held_in)):
        source = source.at[:, c] if target is rec else source
        incoming.append(pltpu.make_async_copy(source, target, arrive.at[n]))
        incoming[-1].start()

    def need(*names):
        for n in names:
            incoming[n].wait()

    begin = [EDGE - REACH + offs[v, 0] for v in range(views)]

    def clear(first, last):
        for v in range(views):

            @pl.loop(first, last)
            def _(e):
                ext[v, e] = jnp.zeros((size, size), F32)

    clear(2 * EDGE + rows, held)

    def along_y(main, halo, x0, base):
        mains, halos = [], []
        for n in range(group):
            mains.append(main(x0 + n))
            halos.append(jnp.concatenate([*halo(x0 + n), zeros_tail], axis=0).T)
        whole = jnp.concatenate([jnp.concatenate(mains, 0), jnp.concatenate(halos, 0)], axis=1)
        done = mm(parts(whole, 1), y_fore[...])
        for v in range(views):
            ext[v, pl.ds(base + x0, group)] = done[:, v * size : (v + 1) * size].reshape(group, size, size)

    need(0)

    @pl.loop(0, rows // group, unroll=2)
    def _(g):
        along_y(
            lambda x: own[:, x].reshape(size, size), lambda x: [edge_l[x], edge_r[x]], g * group, EDGE
        )

    @pl.loop(0, EDGE // group, unroll=3)
    def _(g):
        along_y(lambda x: left[:, x].reshape(size, size), lambda x: [corner_l[x]], g * group, 0)
        along_y(
            lambda x: right[:, x].reshape(size, size), lambda x: [corner_r[x]], g * group, EDGE + rows
        )

    need(1)

    @pl.loop(0, size // (8 * wide), unroll=2)
    def _(n):
        z0 = pl.multiple_of(n * 8 * wide, 8 * wide)
        for v in range(views):
            data = jnp.concatenate(
                [
                    ext[v, pl.ds(begin[v], window), pl.ds(z0 + 8 * k, 8)].reshape(8 * window, size)
                    for k in range(wide)
                ],
                axis=1,
            )
            done = mm(x_fore[v], parts(data, 0))
            for k in range(wide):
                mid[v, :, pl.ds(z0 + 8 * k, 8)] = done[:, k * size : (k + 1) * size].reshape(rows, 8, size)

    need(2, 3, 4)

    @pl.loop(0, rows // group, unroll=2)
    def _(g):
        x0 = g * group
        for v in range(views):
            image = mm(z_fore[v], parts(jnp.concatenate([mid[v, x0 + n] for n in range(group)], axis=1), 0))
            seen = jnp.concatenate([rec[v, x0 + n].astype(F32) for n in range(group)], axis=1)
            back = mm(z_back[v], parts(seen / (image + BACKGROUND), 0))
            for n in range(group):
                mid[v, x0 + n] = back[:, n * size : (n + 1) * size]

    need(5)
    clear(0, EDGE)
    clear(EDGE + rows, 2 * EDGE + rows)

    @pl.loop(0, size // (8 * wide), unroll=2)
    def _(n):
        z0 = pl.multiple_of(n * 8 * wide, 8 * wide)
        for v in range(views):
            data = jnp.concatenate(
                [mid[v, :, pl.ds(z0 + 8 * k, 8)].reshape(8 * rows, size) for k in range(wide)], axis=1
            )
            done = mm(x_back[v], parts(data, 0))
            for k in range(wide):
                ext[v, pl.ds(begin[v], window), pl.ds(z0 + 8 * k, 8)] = done[
                    :, k * size : (k + 1) * size
                ].reshape(window, 8, size)

    need(6)
    leaving = []
    for n, (target, base, count) in enumerate(
        [(v_out.at[0], 0, EDGE), (v_out.at[1], EDGE + rows, EDGE), (out_m, EDGE, rows)]
    ):

        @pl.loop(0, count // group, unroll=3 if count == EDGE else 2)
        def _(g):
            x0 = g * group
            both = [
                jnp.concatenate([ext[v, base + x0 + k] for v in range(views)], axis=1) for k in range(group)
            ]
            done = mm(parts(jnp.concatenate(both, axis=0), 1), y_back[...])
            for k in range(group):
                piece = done[k * size : (k + 1) * size]
                target[x0 + k, :size] = piece[:, :size]
                target[x0 + k, size:] = piece[:, size:].T[: 2 * EDGE]

        if target is not out_m:
            leaving.append(pltpu.make_async_copy(target, (out_l, out_r)[n], depart.at[n]))
            leaving[-1].start()
    for copy in leaving:
        copy.wait()


def correlate(c, offsets, left, own, right, edge_l, edge_r, corner_l, corner_r, rec, tables):
    smem = pl.BlockSpec(memory_space=pltpu.SMEM)
    vmem = pl.BlockSpec(memory_space=pltpu.VMEM)
    hbm = pl.BlockSpec(memory_space=pltpu.HBM)
    rows = own.shape[1]
    views = rec.shape[0]
    tall = LANES + 2 * EDGE
    side = jax.ShapeDtypeStruct((EDGE, tall, LANES), F32)
    y_fore, y_back, z_fore, z_back, x_fore, x_back = tables
    arrays = y_fore, x_fore, rec, z_fore, z_back, x_back, y_back
    count = len(arrays)
    held = [
        pltpu.VMEM((views, rows, LANES, LANES), BF16) if a is rec else pltpu.VMEM(a.shape, a.dtype)
        for a in arrays
    ]
    return pl.pallas_call(
        functools.partial(correlate_kernel, c, count),
        out_shape=(side, jax.ShapeDtypeStruct((rows, tall, LANES), F32), side),
        in_specs=[smem] + [vmem] * 7 + [hbm] * count,
        out_specs=(hbm, vmem, hbm),
        scratch_shapes=held
        + [
            pltpu.VMEM((views, 2 * EDGE + rows + 8, LANES, LANES), F32),
            pltpu.VMEM((views, rows, LANES, LANES), F32),
            pltpu.VMEM((2, EDGE, tall, LANES), F32),
            pltpu.SemaphoreType.DMA((count,)),
            pltpu.SemaphoreType.DMA((2,)),
        ],
        compiler_params=params(46),
        cost_estimate=cost(25),
        name="correlate",
    )(offsets, edge_l, edge_r, own, left, right, corner_l, corner_r, *arrays)


def returning_kernel(own, from_l, from_r, first, last):
    rows, size = own.shape[0], LANES
    for x in range(rows):
        total = own[x, size:]
        if x < EDGE:
            total = total + from_l[x, size:]
        if x >= rows - EDGE:
            total = total + from_r[x - rows + EDGE, size:]
        first[x] = total[:EDGE]
        last[x] = total[EDGE:]


def returning_columns(own, from_l, from_r):
    vmem = pl.BlockSpec(memory_space=pltpu.VMEM)
    edge = jax.ShapeDtypeStruct((own.shape[0], EDGE, LANES), F32)
    return pl.pallas_call(
        returning_kernel,
        in_specs=[vmem] * 3,
        out_specs=(vmem, vmem),
        out_shape=(edge, edge),
        compiler_params=params(),
        cost_estimate=cost(2),
        name="returning_columns",
    )(own, from_l, from_r)


def gather_kernel(own, from_l, from_r, edge_l, edge_r, target):
    rows, size = own.shape[0], LANES
    gap = jnp.zeros((size - 2 * EDGE, size), F32)
    for x in range(rows):
        total = own[x, :size]
        if x < EDGE:
            total = total + from_l[x, :size]
        if x >= rows - EDGE:
            total = total + from_r[x - rows + EDGE, :size]
        total = total + jnp.concatenate([edge_l[x], gap, edge_r[x]], axis=0).T
        target[:, x] = total.reshape(target.shape[0], target.shape[2], size)


def gather_sums(own, from_l, from_r, edge_l, edge_r, peers):
    rows = own.shape[0]
    planes = LANES // peers
    vmem = pl.BlockSpec(memory_space=pltpu.VMEM)
    return pl.pallas_call(
        gather_kernel,
        out_shape=jax.ShapeDtypeStruct((peers, rows, planes, LANES), F32),
        in_specs=[vmem] * 5,
        out_specs=vmem,
        compiler_params=params(),
        cost_estimate=cost(5),
        name="gather_sums",
    )(own, from_l, from_r, edge_l, edge_r)


def update(estimate, spread, c, views, held):
    _, planes, rows, columns = estimate.shape
    peers = spread.shape[0]
    width = columns // peers
    step = min(4, peers)
    block = pl.BlockSpec((1, planes, rows, step * width), lambda s: (c, 0, 0, s))
    extra = [] if held is None else [held]
    return pl.pallas_call(
        functools.partial(update_kernel, views),
        grid=(peers // step,),
        in_specs=[pl.BlockSpec((step, rows, planes, width), lambda s: (s, 0, 0, 0)), block]
        + [pl.BlockSpec(memory_space=pltpu.HBM)] * len(extra),
        out_specs=block,
        out_shape=jax.ShapeDtypeStruct(estimate.shape, F32),
        input_output_aliases={2: 0} if extra else {},
        compiler_params=params(),
        cost_estimate=cost(4),
        name="update",
    )(spread, estimate, *extra)


def update_kernel(views, spread, estimate, *rest):
    width = spread.shape[3]
    for k in range(spread.shape[0]):
        lanes = slice(k * width, (k + 1) * width)
        rest[-1][0, :, :, lanes] = estimate[0, :, :, lanes] * (jnp.swapaxes(spread[k], 0, 1) / views)


def fast_shards(estimate, recorded, psf_lateral, psf_axial, offsets):
    views, colours = recorded.shape[:2]
    rows = estimate.shape[2]
    peers = lax.axis_size("slab")
    lateral = psf_lateral / jnp.sum(psf_lateral, axis=-1, keepdims=True)
    axial = psf_axial / jnp.sum(psf_axial, axis=-1, keepdims=True)
    tables = make_tables(lateral, axial, offsets, rows)
    rec = record_rows(recorded)
    sent = [send_blocks(estimate, c, peers) for c in range(colours)]
    result = None
    pending = None

    def close(c, result, mine, from_l, from_r, back_l, back_r):
        sums = gather_sums(mine, from_l, from_r, back_l, back_r, peers)
        summed = lax.all_to_all(sums, "slab", 0, 0, tiled=True)
        return update(estimate, summed, c, views, result)

    for c in range(colours):
        own = lax.all_to_all(sent[c], "slab", 0, 0, tiled=True)
        if c == 0:
            own, sent, tables, rec = lax.optimization_barrier((own, sent, tables, rec))
        first, last, leading, trailing = block_edges(own)
        edge_l = upward(last, "slab")
        edge_r = downward(first, "slab")
        left = upward(trailing, "view")
        right = downward(leading, "view")
        if c + 1 < colours:
            sent = after(sent, edge_l, edge_r, left, right)
        edges = jnp.concatenate([edge_l, edge_r], axis=1)
        end_l, end_r = edges[rows - EDGE :], edges[:EDGE]
        if pending is not None:
            end_l, end_r, pending = lax.optimization_barrier((end_l, end_r, pending))
            first, last = returning_columns(*pending)
            back_r, back_l = downward(first, "slab"), upward(last, "slab")
        corner_l = upward(end_l, "view")
        corner_r = downward(end_r, "view")
        if pending is not None:
            corner_l, corner_r, first, last = lax.optimization_barrier((corner_l, corner_r, first, last))
        to_l, mine, to_r = correlate(
            c, offsets, left, own, right, edge_l, edge_r, corner_l, corner_r, rec, tables
        )
        if pending is not None:
            mine, back_l, back_r = lax.optimization_barrier((mine, back_l, back_r))
            result = close(c - 1, result, *pending, back_l, back_r)
        pending = mine, upward(to_r, "view"), downward(to_l, "view")
    first, last = returning_columns(*pending)
    return close(colours - 1, result, *pending, upward(last, "slab"), downward(first, "slab"))


def shards(estimate, recorded, psf_lateral, psf_axial, offsets):
    planes, rows, width = recorded.shape[2:]
    fits = planes == LANES and width == LANES and rows % 16 == 0 and rows >= EDGE
    fits = fits and estimate.shape[1] % 16 == 0 and psf_lateral.shape[2] == 2 * REACH + 1
    run = fast_shards if fits else general_shards
    return run(estimate, recorded, psf_lateral, psf_axial, offsets)


def solution(mesh):
    in_specs = (P(None, "slab", "view", None), P(None, None, None, "view", "slab"), P(), P(), P())
    out_specs = P(None, "slab", "view", None)
    return jax.shard_map(shards, mesh=mesh, in_specs=in_specs, out_specs=out_specs, check_vma=False)
```

```python
import functools

import jax
import jax.numpy as jnp
from jax import lax
from jax.experimental import pallas as pl
from jax.experimental.pallas import tpu as pltpu
from jax.sharding import PartitionSpec as P

HALO = 23
BACKGROUND = 0.05
HIGHEST = lax.Precision.HIGHEST
LANES = 128
REACH = 15
EDGE = 24
F32 = jnp.float32
BF16 = jnp.bfloat16


def with_halo(value, sides, width):
    for axis, dim in sides:
        peers, length = (lax.axis_size(axis), value.shape[dim])
        up = [(i, (i + 1) % peers) for i in range(peers - 1)]
        down = [(j, i) for i, j in up]
        last = lax.slice_in_dim(value, length - width, length, axis=dim)
        leading = lax.slice_in_dim(value, 0, width, axis=dim)
        before = lax.ppermute(last, axis, up)
        after = lax.ppermute(leading, axis, down)
        value = jnp.concatenate([before, value, after], axis=dim)
    return value


def unit_taps(weights):
    return weights / jnp.sum(weights)


def band_table(weights, places):
    levels = jnp.arange(weights.shape[0], dtype=jnp.int32)
    return jnp.sum(jnp.where(places[..., None] == levels, weights, 0.0), axis=-1)


def margin_matrix(weights, offset, length, margin, adjoint):
    centre = (weights.shape[0] - 1) // 2
    outputs = jnp.arange(length, dtype=jnp.int32)[:, None]
    sources = jnp.arange(length + 2 * margin, dtype=jnp.int32)[None, :] - margin
    apart = sources - outputs
    if adjoint:
        apart = -apart
    return band_table(weights, apart - offset + centre)


def blocked_rows(field, weights, offset, width_blk, adjoint):
    extent = field.shape
    blocks = extent[3] // width_blk
    pieces = field.reshape(extent[0], extent[1], extent[2], blocks, width_blk)
    padded = jnp.pad(pieces, ((0, 0), (0, 0), (0, 0), (1, 1), (0, 0)))
    centre = (weights.shape[0] - 1) // 2
    sources = jnp.arange(width_blk, dtype=jnp.int32)[:, None]
    outputs = jnp.arange(width_blk, dtype=jnp.int32)[None, :]
    result = jnp.zeros(pieces.shape, F32)
    for shifted in range(3):
        apart = (shifted - 1) * width_blk + sources - outputs
        if adjoint:
            apart = -apart
        matrix = band_table(weights, apart - offset + centre)
        result = result + jnp.einsum(
            "czxkj,ji->czxki",
            padded[:, :, :, shifted : shifted + blocks],
            matrix,
            precision=HIGHEST,
        )
    return result.reshape(extent)


def general_shards(estimate, recorded, psf_lateral, psf_axial, offsets):
    views_n, planes_n = recorded.shape[0], recorded.shape[2]
    along_x = [unit_taps(psf_lateral[which, 0]) for which in range(views_n)]
    along_y = [unit_taps(psf_lateral[which, 1]) for which in range(views_n)]
    rows_at = jnp.arange(planes_n, dtype=jnp.int32)[:, None]
    cols_at = jnp.arange(planes_n, dtype=jnp.int32)[None, :]
    axial_places = cols_at - rows_at + (psf_axial.shape[1] - 1) // 2
    axial = [band_table(unit_taps(psf_axial[which]), axial_places) for which in range(views_n)]
    x_rows = estimate.shape[2]
    widened = with_halo(estimate, (("view", 2),), HALO)
    blurred = []
    for which in range(views_n):
        across = margin_matrix(along_x[which], offsets[which, 0], x_rows, HALO, False)
        sectioned = jnp.einsum("ab,czby->czay", across, widened, precision=HIGHEST)
        blurred.append(blocked_rows(sectioned, along_y[which], offsets[which, 1], LANES, False))
    columns = lax.all_to_all(jnp.stack(blurred), "slab", split_axis=4, concat_axis=2, tiled=True)
    spread = []
    for which in range(views_n):
        imaged = jnp.einsum("oi,cixy->coxy", axial[which], columns[which], precision=HIGHEST)
        quotient = recorded[which].astype(F32) / (imaged + BACKGROUND)
        spread.append(jnp.einsum("oi,coxy->cixy", axial[which], quotient, precision=HIGHEST))
    planes = lax.all_to_all(jnp.stack(spread), "slab", split_axis=2, concat_axis=4, tiled=True)
    returned = [
        blocked_rows(planes[which], along_y[which], offsets[which, 1], LANES, True)
        for which in range(views_n)
    ]
    fringe = with_halo(jnp.stack(returned), (("view", 3),), HALO)
    summed = jnp.zeros(estimate.shape, F32)
    for which in range(views_n):
        across = margin_matrix(along_x[which], offsets[which, 0], x_rows, HALO, True)
        summed = summed + jnp.einsum("ab,czby->czay", across, fringe[which], precision=HIGHEST)
    return estimate * (summed / views_n)


def params(mebibytes=20):
    return pltpu.CompilerParams(vmem_limit_bytes=mebibytes * 1024 * 1024)


def cost(micros):
    return pl.CostEstimate(flops=0, bytes_accessed=int(micros * 3_600_000), transcendentals=0)


def upward(value, axis):
    return lax.ppermute(value, axis, [(i, i + 1) for i in range(lax.axis_size(axis) - 1)])


def downward(value, axis):
    return lax.ppermute(value, axis, [(i + 1, i) for i in range(lax.axis_size(axis) - 1)])


def after(value, *earlier):
    return lax.optimization_barrier((value, earlier))[0]


def split(value):
    high = value.astype(BF16)
    return high, (value - high.astype(F32)).astype(BF16)


def mm(a, b):
    return jnp.dot(a, b, preferred_element_type=F32)


def parts(value, axis):
    high, low = split(value)
    return jnp.concatenate([high, low, high], axis=axis)


def tables_kernel(taps_xy, z_taps, offs, y_fore, y_back, z_fore, z_back, x_fore, x_back, half):
    views, _, taps = taps_xy.shape
    axial = z_taps.shape[1]
    size = LANES
    rows = lax.broadcasted_iota(jnp.int32, (size, size), 0)
    cols = lax.broadcasted_iota(jnp.int32, (size, size), 1)
    halo_row = jnp.where(rows < EDGE, rows - EDGE, rows - EDGE + size)

    def chosen(place, count, tap):
        def step(k, acc):
            return jnp.where(place == k, tap(k), acc)

        return lax.fori_loop(0, count, step, jnp.zeros(place.shape, F32))

    def store(target, value, where):
        high, low = split(value)
        for p, piece in enumerate((high, high, low)):
            target[where(p)] = piece

    def at(r0, c0, height, width):
        return slice(r0, r0 + height), slice(c0, c0 + width)

    for v in range(views):
        shift = offs[v, 1] - (taps - 1) // 2
        for n in range(2):
            place = (rows if n == 0 else halo_row) - cols - shift
            if n == 1:
                place = jnp.where(rows < 2 * EDGE, place, -1)
            fore = chosen(place, taps, lambda k: taps_xy[v, 1, k])
            store(y_fore, fore, lambda p: at((2 * p + n) * size, v * size, size, size))
            store(y_back, fore.T, lambda p: at((views * p + v) * size, n * size, size, size))
        fore = chosen(cols - rows + (axial - 1) // 2, axial, lambda k: z_taps[v, k])
        store(z_fore, fore, lambda p: (v, *at(0, p * size, size, size)))
        store(z_back, fore.T, lambda p: (v, *at(0, p * size, size, size)))

        height, width = x_fore.shape[1], x_fore.shape[2] // 3
        step = 64
        for r0 in range(0, height, step):
            r = lax.broadcasted_iota(jnp.int32, (step, width), 0) + r0
            q = lax.broadcasted_iota(jnp.int32, (step, width), 1)
            place = jnp.where(r % 8 == q % 8, q // 8 - r // 8, -1)
            fore = chosen(place, taps, lambda k: taps_xy[v, 0, k])
            store(x_fore, fore, lambda p: (v, *at(r0, p * width, step, width)))
            half[r0 : r0 + step] = fore
        for r0 in range(0, height, size):
            back = half[r0 : r0 + size].T
            store(x_back, back, lambda p: (v, *at(0, p * height + r0, width, size)))


def make_tables(lateral, axial, offsets, rows):
    smem = pl.BlockSpec(memory_space=pltpu.SMEM)
    vmem = pl.BlockSpec(memory_space=pltpu.VMEM)
    views = lateral.shape[0]
    window = rows + 32
    shapes = [
        (6 * LANES, views * LANES),
        (3 * views * LANES, 2 * LANES),
        (views, LANES, 3 * LANES),
        (views, LANES, 3 * LANES),
        (views, 8 * rows, 3 * 8 * window),
        (views, 8 * window, 3 * 8 * rows),
    ]
    return pl.pallas_call(
        tables_kernel,
        out_shape=tuple(jax.ShapeDtypeStruct(shape, BF16) for shape in shapes),
        in_specs=[smem] * 3,
        out_specs=(vmem,) * len(shapes),
        compiler_params=params(),
        scratch_shapes=[pltpu.VMEM((8 * rows, 8 * window), F32)],
        cost_estimate=cost(14),
        name="tables",
    )(lateral, axial, offsets)


def swap_kernel(source, target):
    width = target.shape[3]
    for k in range(target.shape[0]):
        target[k] = jnp.swapaxes(source[0, :, :, k * width : (k + 1) * width], 0, 1)


def send_blocks(estimate, c, peers):
    _, planes, rows, columns = estimate.shape
    width = columns // peers
    step = min(4, peers)
    return pl.pallas_call(
        swap_kernel,
        grid=(peers // step,),
        in_specs=[pl.BlockSpec((1, planes, rows, step * width), lambda s: (c, 0, 0, s))],
        out_specs=pl.BlockSpec((step, rows, planes, width), lambda s: (s, 0, 0, 0)),
        out_shape=jax.ShapeDtypeStruct((peers, rows, planes, width), F32),
        compiler_params=params(),
        cost_estimate=cost(3),
        name="send_blocks",
    )(estimate)


def record_kernel(source, target):
    target[0, 0] = jnp.swapaxes(source[0, 0].astype(F32), 0, 1).astype(BF16)


def record_rows(recorded):
    views, colours, planes, rows, width = recorded.shape
    step = 64
    return pl.pallas_call(
        record_kernel,
        grid=(views, colours, planes // step),
        in_specs=[pl.BlockSpec((1, 1, step, rows, width), lambda v, c, z: (v, c, z, 0, 0))],
        out_specs=pl.BlockSpec((1, 1, rows, step, width), lambda v, c, z: (v, c, 0, z, 0)),
        out_shape=jax.ShapeDtypeStruct((views, colours, rows, planes, width), BF16),
        compiler_params=params(),
        cost_estimate=cost(8),
        name="record_rows",
    )(recorded)


def edges_kernel(block, first, last, leading, trailing, sems):
    peers, rows, planes, size = block.shape
    depart = [
        pltpu.make_async_copy(block.at[:, pl.ds(0, EDGE)], leading, sems.at[0]),
        pltpu.make_async_copy(block.at[:, pl.ds(rows - EDGE, EDGE)], trailing, sems.at[1]),
    ]
    for copy in depart:
        copy.start()
    for x in range(rows):
        turned = block[:, x].reshape(peers * planes, size).T
        first[x] = turned[:EDGE]
        last[x] = turned[-EDGE:]
    for copy in depart:
        copy.wait()


def block_edges(block):
    peers, rows, planes, width = block.shape
    hbm = pl.BlockSpec(memory_space=pltpu.HBM)
    vmem = pl.BlockSpec(memory_space=pltpu.VMEM)
    edge = jax.ShapeDtypeStruct((rows, EDGE, peers * planes), F32)
    side = jax.ShapeDtypeStruct((peers, EDGE, planes, width), F32)
    return pl.pallas_call(
        edges_kernel,
        in_specs=[vmem],
        out_specs=(vmem, vmem, hbm, hbm),
        out_shape=(edge, edge, side, side),
        scratch_shapes=[pltpu.SemaphoreType.DMA((2,))],
        compiler_params=params(),
        cost_estimate=cost(4),
        name="block_edges",
    )(block)


def correlate_kernel(c, count, offs, edge_l, edge_r, own, left, right, corner_l, corner_r, *rest):
    sources, rest = rest[:count], rest[count:]
    (out_l, out_m, out_r), held_in, rest = rest[:3], rest[3 : 3 + count], rest[3 + count :]
    ext, mid, v_out, arrive, depart = rest
    y_fore, x_fore, rec, z_fore, z_back, x_back, y_back = held_in
    views = rec.shape[0]
    rows = own.shape[1]
    size = LANES
    window = x_back.shape[1] // 8
    group = 8
    wide = 4
    held = ext.shape[1]
    zeros_tail = jnp.zeros((size - 2 * EDGE, size), F32)
    incoming = []
    for n, (source, target) in enumerate(zip(sources, held_in)):
        source = source.at[:, c] if target is rec else source
        incoming.append(pltpu.make_async_copy(source, target, arrive.at[n]))
        incoming[-1].start()

    def need(*names):
        for n in names:
            incoming[n].wait()

    begin = [EDGE - REACH + offs[v, 0] for v in range(views)]

    def clear(first, last):
        for v in range(views):

            @pl.loop(first, last)
            def _(e):
                ext[v, e] = jnp.zeros((size, size), F32)

    clear(2 * EDGE + rows, held)

    def along_y(main, halo, x0, base):
        mains, halos = [], []
        for n in range(group):
            mains.append(main(x0 + n))
            halos.append(jnp.concatenate([*halo(x0 + n), zeros_tail], axis=0).T)
        whole = jnp.concatenate([jnp.concatenate(mains, 0), jnp.concatenate(halos, 0)], axis=1)
        done = mm(parts(whole, 1), y_fore[...])
        for v in range(views):
            ext[v, pl.ds(base + x0, group)] = done[:, v * size : (v + 1) * size].reshape(group, size, size)

    need(0)

    @pl.loop(0, rows // group, unroll=2)
    def _(g):
        along_y(
            lambda x: own[:, x].reshape(size, size), lambda x: [edge_l[x], edge_r[x]], g * group, EDGE
        )

    @pl.loop(0, EDGE // group, unroll=3)
    def _(g):
        along_y(lambda x: left[:, x].reshape(size, size), lambda x: [corner_l[x]], g * group, 0)
        along_y(
            lambda x: right[:, x].reshape(size, size), lambda x: [corner_r[x]], g * group, EDGE + rows
        )

    need(1)

    @pl.loop(0, size // (8 * wide), unroll=2)
    def _(n):
        z0 = pl.multiple_of(n * 8 * wide, 8 * wide)
        for v in range(views):
            data = jnp.concatenate(
                [
                    ext[v, pl.ds(begin[v], window), pl.ds(z0 + 8 * k, 8)].reshape(8 * window, size)
                    for k in range(wide)
                ],
                axis=1,
            )
            done = mm(x_fore[v], parts(data, 0))
            for k in range(wide):
                mid[v, :, pl.ds(z0 + 8 * k, 8)] = done[:, k * size : (k + 1) * size].reshape(rows, 8, size)

    need(2, 3, 4)

    @pl.loop(0, rows // group, unroll=2)
    def _(g):
        x0 = g * group
        for v in range(views):
            image = mm(z_fore[v], parts(jnp.concatenate([mid[v, x0 + n] for n in range(group)], axis=1), 0))
            seen = jnp.concatenate([rec[v, x0 + n].astype(F32) for n in range(group)], axis=1)
            back = mm(z_back[v], parts(seen / (image + BACKGROUND), 0))
            for n in range(group):
                mid[v, x0 + n] = back[:, n * size : (n + 1) * size]

    need(5)
    clear(0, EDGE)
    clear(EDGE + rows, 2 * EDGE + rows)

    @pl.loop(0, size // (8 * wide), unroll=2)
    def _(n):
        z0 = pl.multiple_of(n * 8 * wide, 8 * wide)
        for v in range(views):
            data = jnp.concatenate(
                [mid[v, :, pl.ds(z0 + 8 * k, 8)].reshape(8 * rows, size) for k in range(wide)], axis=1
            )
            done = mm(x_back[v], parts(data, 0))
            for k in range(wide):
                ext[v, pl.ds(begin[v], window), pl.ds(z0 + 8 * k, 8)] = done[
                    :, k * size : (k + 1) * size
                ].reshape(window, 8, size)

    need(6)
    leaving = []
    for n, (target, base, count) in enumerate(
        [(v_out.at[0], 0, EDGE), (v_out.at[1], EDGE + rows, EDGE), (out_m, EDGE, rows)]
    ):

        @pl.loop(0, count // group, unroll=3 if count == EDGE else 2)
        def _(g):
            x0 = g * group
            both = [
                jnp.concatenate([ext[v, base + x0 + k] for v in range(views)], axis=1) for k in range(group)
            ]
            done = mm(parts(jnp.concatenate(both, axis=0), 1), y_back[...])
            for k in range(group):
                piece = done[k * size : (k + 1) * size]
                target[x0 + k, :size] = piece[:, :size]
                target[x0 + k, size:] = piece[:, size:].T[: 2 * EDGE]

        if target is not out_m:
            leaving.append(pltpu.make_async_copy(target, (out_l, out_r)[n], depart.at[n]))
            leaving[-1].start()
    for copy in leaving:
        copy.wait()


def correlate(c, offsets, left, own, right, edge_l, edge_r, corner_l, corner_r, rec, tables):
    smem = pl.BlockSpec(memory_space=pltpu.SMEM)
    vmem = pl.BlockSpec(memory_space=pltpu.VMEM)
    hbm = pl.BlockSpec(memory_space=pltpu.HBM)
    rows = own.shape[1]
    views = rec.shape[0]
    tall = LANES + 2 * EDGE
    side = jax.ShapeDtypeStruct((EDGE, tall, LANES), F32)
    y_fore, y_back, z_fore, z_back, x_fore, x_back = tables
    arrays = y_fore, x_fore, rec, z_fore, z_back, x_back, y_back
    count = len(arrays)
    held = [
        pltpu.VMEM((views, rows, LANES, LANES), BF16) if a is rec else pltpu.VMEM(a.shape, a.dtype)
        for a in arrays
    ]
    return pl.pallas_call(
        functools.partial(correlate_kernel, c, count),
        out_shape=(side, jax.ShapeDtypeStruct((rows, tall, LANES), F32), side),
        in_specs=[smem] + [vmem] * 7 + [hbm] * count,
        out_specs=(hbm, vmem, hbm),
        scratch_shapes=held
        + [
            pltpu.VMEM((views, 2 * EDGE + rows + 8, LANES, LANES), F32),
            pltpu.VMEM((views, rows, LANES, LANES), F32),
            pltpu.VMEM((2, EDGE, tall, LANES), F32),
            pltpu.SemaphoreType.DMA((count,)),
            pltpu.SemaphoreType.DMA((2,)),
        ],
        compiler_params=params(46),
        cost_estimate=cost(25),
        name="correlate",
    )(offsets, edge_l, edge_r, own, left, right, corner_l, corner_r, *arrays)


def returning_kernel(own, from_l, from_r, first, last):
    rows, size = own.shape[0], LANES
    for x in range(rows):
        total = own[x, size:]
        if x < EDGE:
            total = total + from_l[x, size:]
        if x >= rows - EDGE:
            total = total + from_r[x - rows + EDGE, size:]
        first[x] = total[:EDGE]
        last[x] = total[EDGE:]


def returning_columns(own, from_l, from_r):
    vmem = pl.BlockSpec(memory_space=pltpu.VMEM)
    edge = jax.ShapeDtypeStruct((own.shape[0], EDGE, LANES), F32)
    return pl.pallas_call(
        returning_kernel,
        in_specs=[vmem] * 3,
        out_specs=(vmem, vmem),
        out_shape=(edge, edge),
        compiler_params=params(),
        cost_estimate=cost(2),
        name="returning_columns",
    )(own, from_l, from_r)


def gather_kernel(own, from_l, from_r, edge_l, edge_r, target):
    rows, size = own.shape[0], LANES
    gap = jnp.zeros((size - 2 * EDGE, size), F32)
    for x in range(rows):
        total = own[x, :size]
        if x < EDGE:
            total = total + from_l[x, :size]
        if x >= rows - EDGE:
            total = total + from_r[x - rows + EDGE, :size]
        total = total + jnp.concatenate([edge_l[x], gap, edge_r[x]], axis=0).T
        target[:, x] = total.reshape(target.shape[0], target.shape[2], size)


def gather_sums(own, from_l, from_r, edge_l, edge_r, peers):
    rows = own.shape[0]
    planes = LANES // peers
    vmem = pl.BlockSpec(memory_space=pltpu.VMEM)
    return pl.pallas_call(
        gather_kernel,
        out_shape=jax.ShapeDtypeStruct((peers, rows, planes, LANES), F32),
        in_specs=[vmem] * 5,
        out_specs=vmem,
        compiler_params=params(),
        cost_estimate=cost(5),
        name="gather_sums",
    )(own, from_l, from_r, edge_l, edge_r)


def update(estimate, spread, c, views, held):
    _, planes, rows, columns = estimate.shape
    peers = spread.shape[0]
    width = columns // peers
    step = min(4, peers)
    block = pl.BlockSpec((1, planes, rows, step * width), lambda s: (c, 0, 0, s))
    extra = [] if held is None else [held]
    return pl.pallas_call(
        functools.partial(update_kernel, views),
        grid=(peers // step,),
        in_specs=[pl.BlockSpec((step, rows, planes, width), lambda s: (s, 0, 0, 0)), block]
        + [pl.BlockSpec(memory_space=pltpu.HBM)] * len(extra),
        out_specs=block,
        out_shape=jax.ShapeDtypeStruct(estimate.shape, F32),
        input_output_aliases={2: 0} if extra else {},
        compiler_params=params(60),
        cost_estimate=cost(4),
        name="update",
    )(spread, estimate, *extra)


def update_kernel(views, spread, estimate, *rest):
    width = spread.shape[3]
    for k in range(spread.shape[0]):
        lanes = slice(k * width, (k + 1) * width)
        rest[-1][0, :, :, lanes] = estimate[0, :, :, lanes] * (jnp.swapaxes(spread[k], 0, 1) / views)


def fast_shards(estimate, recorded, psf_lateral, psf_axial, offsets):
    views, colours = recorded.shape[:2]
    rows = estimate.shape[2]
    peers = lax.axis_size("slab")
    lateral = psf_lateral / jnp.sum(psf_lateral, axis=-1, keepdims=True)
    axial = psf_axial / jnp.sum(psf_axial, axis=-1, keepdims=True)
    tables = make_tables(lateral, axial, offsets, rows)
    rec = record_rows(recorded)
    sent = [send_blocks(estimate, c, peers) for c in range(colours)]
    result = None
    pending = None

    def close(c, result, mine, from_l, from_r, back_l, back_r):
        sums = gather_sums(mine, from_l, from_r, back_l, back_r, peers)
        summed = lax.all_to_all(sums, "slab", 0, 0, tiled=True)
        return update(estimate, summed, c, views, result)

    for c in range(colours):
        own = lax.all_to_all(sent[c], "slab", 0, 0, tiled=True)
        if c == 0:
            own, sent, tables, rec = lax.optimization_barrier((own, sent, tables, rec))
        first, last, leading, trailing = block_edges(own)
        edge_l = upward(last, "slab")
        edge_r = downward(first, "slab")
        left = upward(trailing, "view")
        right = downward(leading, "view")
        if c + 1 < colours:
            sent = after(sent, edge_l, edge_r, left, right)
        edges = jnp.concatenate([edge_l, edge_r], axis=1)
        end_l, end_r = edges[rows - EDGE :], edges[:EDGE]
        if pending is not None:
            end_l, end_r, pending = lax.optimization_barrier((end_l, end_r, pending))
            first, last = returning_columns(*pending)
            back_r, back_l = downward(first, "slab"), upward(last, "slab")
        corner_l = upward(end_l, "view")
        corner_r = downward(end_r, "view")
        if pending is not None:
            corner_l, corner_r, first, last = lax.optimization_barrier((corner_l, corner_r, first, last))
        to_l, mine, to_r = correlate(
            c, offsets, left, own, right, edge_l, edge_r, corner_l, corner_r, rec, tables
        )
        if pending is not None:
            mine, back_l, back_r = lax.optimization_barrier((mine, back_l, back_r))
            result = close(c - 1, result, *pending, back_l, back_r)
        pending = mine, upward(to_r, "view"), downward(to_l, "view")
    first, last = returning_columns(*pending)
    return close(colours - 1, result, *pending, upward(last, "slab"), downward(first, "slab"))


def shards(estimate, recorded, psf_lateral, psf_axial, offsets):
    planes, rows, width = recorded.shape[2:]
    fits = planes == LANES and width == LANES and rows % 16 == 0 and rows >= EDGE
    fits = fits and estimate.shape[1] % 16 == 0 and psf_lateral.shape[2] == 2 * REACH + 1
    run = fast_shards if fits else general_shards
    return run(estimate, recorded, psf_lateral, psf_axial, offsets)


def solution(mesh):
    in_specs = (P(None, "slab", "view", None), P(None, None, None, "view", "slab"), P(), P(), P())
    out_specs = P(None, "slab", "view", None)
    return jax.shard_map(shards, mesh=mesh, in_specs=in_specs, out_specs=out_specs, check_vma=False)
```
